256 devices in a mesh: ctx: 128 (over y, z, x), head: 2 (over core).
Axes of the slice: x: 4, y: 4, z: 8, core: 2. Of those that a mesh axis runs over, the one named last changes fastest.
Arguments:
- queries: bfloat16 [32768, 1024], P('ctx', 'head'), may hold values from -2.5 to 2.5
- keys: bfloat16 [32768, 1024], P('ctx', 'head'), may hold values from -2.5 to 2.5
- values: bfloat16 [32768, 1024], P('ctx', 'head'), may hold values from -6 to 6
- log_decay: float32 [8, 32768], P('head', 'ctx'), may hold values from -0.75 to 0, as said below
- out_weight: bfloat16 [1024, 2048], P('head'), may hold values from -0.1875 to 0.1875
- out_grad: bfloat16 [32768, 2048], P('ctx', 'head'), may hold values from -6 to 6
Outputs:
- mixed: bfloat16 [32768, 2048], P('ctx', 'head')
- grad_queries: bfloat16 [32768, 1024], P('ctx', 'head')
- grad_keys: bfloat16 [32768, 1024], P('ctx', 'head')
- grad_values: bfloat16 [32768, 1024], P('ctx', 'head')
The draws below stay inside these ranges and needn't reach their ends.
Inputs may be any that keep to these rules, and one draw needn't show every extreme that they name: log_decay is negative everywhere.
All inputs are finite; a program needn't handle non-finite values.
Results may differ from the reference program's by a relative error of at most 0.018.
Values may be sent and summed in bfloat16 or wider, within the bound.
No kernel may reach another device: no remote copies, remote signals or barrier semaphores. Data moves between devices by JAX's collectives and lax.ppermute only.
A program may use at most 128 MiB of HBM per device.

```python
import math
import jax
import jax.numpy as jnp
from jax import lax

D = 2048
HEAD_TOTAL = 8
DK = 128
DV = 128
SPAN = 256
TOKEN_TOTAL = 32768


def draw_log_decay(key, part):
    parallel_sequences = jax.random.split(key, 7)
    fast_share = 0.5
    head_draw = jax.random.uniform(parallel_sequences[0], (HEAD_TOTAL,))
    fast_heads = head_draw < fast_share
    slow_rate = jnp.exp(jax.random.uniform(parallel_sequences[1], (HEAD_TOTAL,), jnp.float32, math.log(0.1), math.log(0.6))) / TOKEN_TOTAL
    fast_rate = jnp.exp(jax.random.uniform(parallel_sequences[2], (HEAD_TOTAL,), jnp.float32, math.log(0.011), math.log(0.023)))
    base_rate = jnp.where(fast_heads, fast_rate, slow_rate)
    token_factor = jnp.exp(jax.random.uniform(parallel_sequences[3], (HEAD_TOTAL, TOKEN_TOTAL), jnp.float32, math.log(0.25), math.log(4.0)))
    block_factor = jnp.exp(jax.random.uniform(parallel_sequences[4], (HEAD_TOTAL, TOKEN_TOTAL // SPAN), jnp.float32, math.log(0.5), math.log(2.0)))
    block_factor = jnp.repeat(block_factor, SPAN, axis=1)
    gentle_component = -base_rate[:, None] * token_factor * block_factor
    spike_locations = jax.random.randint(parallel_sequences[5], (HEAD_TOTAL, 2), 0, TOKEN_TOTAL)
    token_positions = jnp.arange(TOKEN_TOTAL)
    spike_match = jnp.any(token_positions[None, None, :] == spike_locations[:, :, None], axis=1)
    spike_magnitude = jax.random.uniform(parallel_sequences[6], (HEAD_TOTAL, TOKEN_TOTAL), jnp.float32, 0.2, 0.4)
    return jnp.where(spike_match, gentle_component + jnp.log1p(-spike_magnitude), gentle_component).astype(jnp.float32)


def block_levels(rng, shape, shards, smallest, top_value):
    gain, own = 1.0, jax.random.fold_in(rng, 6)
    for position, blocks in shards:
        heights = jnp.exp(jax.random.uniform(jax.random.fold_in(own, position), (blocks,), jnp.float32, smallest / len(shards), top_value / len(shards)))
        gain = gain * jnp.repeat(heights, shape[position] // blocks).reshape([-1 if axis == position else 1 for axis in range(len(shape))])
    return gain


def scatter_about(rng, shape, deviation, bound, shards=(), kind=jnp.bfloat16):
    result = deviation * jax.random.normal(rng, shape, jnp.float32)
    if shards:
        result = result * block_levels(rng, shape, shards, -0.22, 0.18)
    return jnp.clip(result, -bound, bound).astype(kind)


def setup_inputs(seed: int = 0) -> dict:
    key_of = jax.random.split(jax.random.key(seed), 7)
    return {
        "queries": scatter_about(key_of[0], (TOKEN_TOTAL, HEAD_TOTAL * DK), 0.3, 2.5, ((0, 128), (1, 2))),
        "keys": scatter_about(key_of[1], (TOKEN_TOTAL, HEAD_TOTAL * DK), 0.3, 2.5, ((0, 128), (1, 2))),
        "values": scatter_about(key_of[2], (TOKEN_TOTAL, HEAD_TOTAL * DV), 1.0, 6.0, ((0, 128), (1, 2))),
        "log_decay": draw_log_decay(jax.random.fold_in(key_of[6], 71), 0),
        "out_weight": scatter_about(key_of[4], (HEAD_TOTAL * DV, D), (HEAD_TOTAL * DV) ** -0.5, 0.1875, ((0, 2),)),
        "out_grad": scatter_about(key_of[5], (TOKEN_TOTAL, D), 1.0, 6.0, ((0, 128), (1, 2))),
    }


epsilon = 1e-05

def block_terms(query_block, key_block, decay_block):
    token_positions = jnp.arange(SPAN)
    causal = token_positions[:, None] >= token_positions[None, :]
    cumulative = jnp.cumsum(decay_block)
    decay_mask = jnp.where(causal, jnp.exp(jnp.minimum(cumulative[:, None] - cumulative[None, :], 0.0)), 0.0)
    scores = jnp.dot(query_block, key_block.T, preferred_element_type=jnp.float32)
    return (cumulative, decay_mask, (scores * decay_mask).astype(jnp.bfloat16))

def forward_block(state, pieces):
    query_block, key_block, value_block, decay_block = pieces
    cumulative, decay_mask, attn_probs = block_terms(query_block, key_block, decay_block)
    state_bf = state.astype(jnp.bfloat16)
    attended = jnp.dot(attn_probs, value_block, preferred_element_type=jnp.float32) + jnp.exp(cumulative)[:, None] * jnp.dot(query_block, state_bf, preferred_element_type=jnp.float32)
    key_weighted = (key_block * jnp.exp(cumulative[-1] - cumulative)[:, None]).astype(jnp.bfloat16)
    new_state = jnp.exp(cumulative[-1]) * state + jnp.dot(key_weighted.T, value_block, preferred_element_type=jnp.float32)
    return (new_state, (attended, state))

def backward_block(grad_state, pieces):
    query_block, key_block, value_block, decay_block, grad_block, state = pieces
    cumulative, decay_mask, attn_probs = block_terms(query_block, key_block, decay_block)
    state_bf = state.astype(jnp.bfloat16)
    grad_bf = grad_state.astype(jnp.bfloat16)
    d_probs = jnp.dot(grad_block, value_block.T, preferred_element_type=jnp.float32)
    d_scores = (d_probs * decay_mask).astype(jnp.bfloat16)
    growth = jnp.exp(cumulative)[:, None]
    weight_key = jnp.exp(cumulative[-1] - cumulative)[:, None]
    grad_query = jnp.dot(d_scores, key_block, preferred_element_type=jnp.float32) + growth * jnp.dot(grad_block, state_bf.T, preferred_element_type=jnp.float32)
    grad_key = jnp.dot(d_scores.T, query_block, preferred_element_type=jnp.float32) + weight_key * jnp.dot(value_block, grad_bf.T, preferred_element_type=jnp.float32)
    grad_value = jnp.dot(attn_probs.T, grad_block, preferred_element_type=jnp.float32) + weight_key * jnp.dot(key_block, grad_bf, preferred_element_type=jnp.float32)
    query_weighted = (query_block * growth).astype(jnp.bfloat16)
    new_grad = jnp.exp(cumulative[-1]) * grad_state + jnp.dot(query_weighted.T, grad_block, preferred_element_type=jnp.float32)
    return (new_grad, (grad_query, grad_key, grad_value))

def one_head(inputs):
    query_h, key_h, value_h, decay_h, grad_h = inputs
    blocks = query_h.shape[0] // SPAN
    shaped = (query_h.reshape(blocks, SPAN, DK), key_h.reshape(blocks, SPAN, DK), value_h.reshape(blocks, SPAN, DV), decay_h.reshape(blocks, SPAN))
    zero_state = jnp.zeros((DK, DV), jnp.float32)
    unused, (attended, state_in) = lax.scan(forward_block, zero_state, shaped)
    attended = attended.reshape(-1, DV)
    inv_rms = lax.rsqrt(lax.optimization_barrier(jnp.mean(attended * attended, axis=1)) + epsilon)
    normed = (attended * inv_rms[:, None]).astype(jnp.bfloat16)
    grad_att = inv_rms[:, None] * grad_h - attended * (inv_rms ** 3 * lax.optimization_barrier(jnp.mean(grad_h * attended, axis=1)))[:, None]
    grad_bf = grad_att.astype(jnp.bfloat16).reshape(blocks, SPAN, DV)
    unused_grad, (grad_query, grad_key, grad_value) = lax.scan(backward_block, zero_state, shaped + (grad_bf, state_in), reverse=True)
    return (normed, grad_query.reshape(-1, DK), grad_key.reshape(-1, DK), grad_value.reshape(-1, DV))

def reference(queries, keys, values, log_decay, out_weight, out_grad):
    tokens = queries.shape[0]
    grad_norm = jnp.dot(out_grad, out_weight.T, preferred_element_type=jnp.float32)

    def by_head(matrix, width):
        return jnp.transpose(matrix.reshape(tokens, HEAD_TOTAL, width), (1, 0, 2))

    def by_token(stacked):
        return jnp.transpose(stacked, (1, 0, 2)).reshape(tokens, -1)
    normed, grad_query, grad_key, grad_value = lax.map(one_head, (by_head(queries, DK), by_head(keys, DK), by_head(values, DV), log_decay, by_head(grad_norm, DV)))
    mixed = jnp.dot(by_token(normed), out_weight, preferred_element_type=jnp.float32).astype(jnp.bfloat16)
    return (mixed, by_token(grad_query).astype(jnp.bfloat16), by_token(grad_key).astype(jnp.bfloat16), by_token(grad_value).astype(jnp.bfloat16))
```

```python
import functools

import jax
import jax.numpy as jnp
from jax import lax
from jax.experimental import pallas as pl
from jax.experimental.pallas import tpu as pltpu
from jax.sharding import PartitionSpec as P

EPS = 1e-05
F32 = jnp.float32
BF = jnp.bfloat16
W = 128


def dot(a, b, da=1, db=0, precision=None):
    return lax.dot_general(
        a, b, (((da,), (db,)), ((), ())), preferred_element_type=F32, precision=precision
    )


def call(body, outs, *args, flops=0, smem=0):
    spec = [pl.BlockSpec(memory_space=pltpu.SMEM)] * smem
    spec += [pl.BlockSpec(memory_space=pltpu.VMEM)] * (len(args) - smem)
    moved = sum(a.size * a.dtype.itemsize for a in (*args, *outs))
    return pl.pallas_call(
        body,
        out_shape=outs,
        in_specs=spec,
        out_specs=[pl.BlockSpec(memory_space=pltpu.VMEM)] * len(outs),
        cost_estimate=pl.CostEstimate(flops=flops, bytes_accessed=moved, transcendentals=0),
        name=body.__name__ if hasattr(body, "__name__") else body.func.__name__,
    )(*args)


def shape(*dims, dtype=BF):
    return jax.ShapeDtypeStruct(dims, dtype)


def head_cols(h):
    return slice(h * W, (h + 1) * W)


def spread(ref, h, matrix, per):
    for r in range(matrix.shape[0] // per):
        ref[h * per : (h + 1) * per, r * W : (r + 1) * W] = matrix[r * per : (r + 1) * per].astype(ref.dtype)


def collect(ref, h, per):
    return jnp.concatenate(
        [ref[h * per : (h + 1) * per, r * W : (r + 1) * W] for r in range(W // per)], axis=0
    )


def block_delta(k_ref, v_ref, ld_ref, pay_ref, col_ref, row_ref):
    heads, span = ld_ref.shape
    per = pay_ref.shape[0] // heads
    ld = ld_ref[...]
    a = lax.broadcasted_iota(jnp.int32, (span, span), 0)
    b = lax.broadcasted_iota(jnp.int32, (span, span), 1)
    row = dot(ld, (a <= b).astype(F32), precision=lax.Precision.HIGHEST)
    col = dot((b <= a).astype(F32), ld, 1, 1, precision=lax.Precision.HIGHEST)
    row_ref[...] = row
    last = col[span - 1 : span, :]
    col_ref[0] = jnp.exp(col)
    weight = jnp.exp(last - col)
    col_ref[1] = weight
    col_ref[2] = col
    lane = lax.broadcasted_iota(jnp.int32, (per, W), 1)
    for h in range(heads):
        kw = (k_ref[:, head_cols(h)].astype(F32) * weight[:, h : h + 1]).astype(BF)
        spread(pay_ref, h, dot(kw, v_ref[:, head_cols(h)], 0, 0), per)
        end = jnp.broadcast_to(last[:, h : h + 1], (per, W))
        hi = end.astype(BF).astype(F32)
        mid = (end - hi).astype(BF).astype(F32)
        low = end - hi - mid
        tail = jnp.where(lane == 0, hi, jnp.where(lane == 1, mid, jnp.where(lane == 2, low, 0.0)))
        pay_ref[h * per : (h + 1) * per, W * W // per :] = tail.astype(BF)


def inside(q_ref, k_ref, v_ref, col_ref, row_ref, probs_ref, mask_ref, in_ref):
    heads, span = row_ref.shape
    a = lax.broadcasted_iota(jnp.int32, (span, span), 0)
    b = lax.broadcasted_iota(jnp.int32, (span, span), 1)
    for h in range(heads):
        gap = col_ref[2][:, h : h + 1] - row_ref[h : h + 1, :]
        mask = jnp.where(b <= a, jnp.exp(jnp.minimum(gap, 0.0)), 0.0)
        mask_ref[h] = mask
        probs = (dot(q_ref[:, head_cols(h)], k_ref[:, head_cols(h)], 1, 1) * mask).astype(BF)
        probs_ref[h] = probs
        in_ref[:, head_cols(h)] = dot(probs, v_ref[:, head_cols(h)])


def grad_of_norm(core_ref, own_ref, other_ref, w_ref, out_ref):
    width = own_ref.shape[1]
    mine = pl.multiple_of(core_ref[0] * width, width)
    theirs = pl.multiple_of((1 - core_ref[0]) * width, width)
    out_ref[...] = dot(own_ref[...], w_ref[:, pl.ds(mine, width)], 1, 1) + dot(
        other_ref[...], w_ref[:, pl.ds(theirs, width)], 1, 1
    )


def forward_scan(x_ref, y_ref, mh_ref, ml_ref):
    count, width = y_ref.shape
    i = lax.broadcasted_iota(jnp.int32, (count, count), 0)
    j = lax.broadcasted_iota(jnp.int32, (count, count), 1)
    before = (j < i).astype(BF)
    gap = jnp.zeros((count, count), F32)
    for piece in range(3):
        end = x_ref[:, width + piece : width + piece + 1].astype(F32)
        gap = gap + dot(before, jnp.where(j < i, end, 0.0).astype(BF))
    reach = jnp.where(j < i, jnp.exp(jnp.minimum(gap, 0.0)), 0.0)
    high = reach.astype(BF)
    low = (reach - high.astype(F32)).astype(BF)
    mh_ref[...] = high
    ml_ref[...] = low
    x = x_ref[:, :width]
    y_ref[...] = (dot(high, x) + dot(low, x)).astype(BF)


def backward_scan(x_ref, mh_ref, ml_ref, y_ref):
    x = x_ref[...]
    y_ref[...] = (dot(mh_ref[...], x, 0, 0) + dot(ml_ref[...], x, 0, 0)).astype(BF)


def norm_and_grad(q_ref, s_ref, col_ref, in_ref, gn_ref, normed_ref, g_ref, pay_ref):
    heads = in_ref.shape[1] // W
    per = s_ref.shape[0] // heads
    for h in range(heads):
        cols = head_cols(h)
        growth = col_ref[0][:, h : h + 1]
        q = q_ref[:, cols]
        att = in_ref[:, cols] + growth * dot(q, collect(s_ref, h, per))
        inv = lax.rsqrt(jnp.mean(att * att, axis=1, keepdims=True) + EPS)
        normed_ref[:, cols] = (att * inv).astype(BF)
        gn = gn_ref[:, cols]
        g = inv * gn - att * (inv * inv * inv * jnp.mean(gn * att, axis=1, keepdims=True))
        g = g.astype(BF)
        g_ref[:, cols] = g
        spread(pay_ref, h, dot((q.astype(F32) * growth).astype(BF), g, 0, 0), per)


def mix(core_ref, normed_ref, w_ref, own_ref, other_ref):
    width = own_ref.shape[1]
    mine = pl.multiple_of(core_ref[0] * width, width)
    theirs = pl.multiple_of((1 - core_ref[0]) * width, width)
    other_ref[...] = dot(normed_ref[...], w_ref[:, pl.ds(theirs, width)]).astype(BF)
    own_ref[...] = dot(normed_ref[...], w_ref[:, pl.ds(mine, width)])


def score_grads(q_ref, k_ref, v_ref, g_ref, s_ref, col_ref, probs_ref, mask_ref, gq_ref, gk_ref, gv_ref):
    heads = probs_ref.shape[0]
    per = s_ref.shape[0] // heads
    for h in range(heads):
        cols = head_cols(h)
        g = g_ref[:, cols]
        d = (dot(g, v_ref[:, cols], 1, 1) * mask_ref[h]).astype(BF)
        carried = dot(g, collect(s_ref, h, per), 1, 1)
        gq_ref[:, cols] = (dot(d, k_ref[:, cols]) + col_ref[0][:, h : h + 1] * carried).astype(BF)
        gk_ref[:, cols] = dot(d, q_ref[:, cols], 0, 0)
        gv_ref[:, cols] = dot(probs_ref[h], g, 0, 0)


def finish(k_ref, v_ref, e_ref, col_ref, gkp_ref, gvp_ref, gk_ref, gv_ref):
    heads = gk_ref.shape[1] // W
    per = e_ref.shape[0] // heads
    for h in range(heads):
        cols = head_cols(h)
        weight = col_ref[1][:, h : h + 1]
        e = collect(e_ref, h, per)
        gk_ref[:, cols] = (gkp_ref[:, cols] + weight * dot(v_ref[:, cols], e, 1, 1)).astype(BF)
        gv_ref[:, cols] = (gvp_ref[:, cols] + weight * dot(k_ref[:, cols], e)).astype(BF)


def local(queries, keys, values, log_decay, out_weight, out_grad):
    rows, width = queries.shape
    heads, span = log_decay.shape
    count = lax.axis_size("ctx")
    slots = heads * W * W // count
    model = out_weight.shape[1]
    core = lax.axis_index("head").astype(jnp.int32).reshape(1)
    swap = [(0, 1), (1, 0)]

    other_grad = lax.ppermute(out_grad, "head", swap)
    pay, col, row = call(
        block_delta,
        [shape(count, slots + W), shape(3, rows, heads, dtype=F32), shape(heads, span, dtype=F32)],
        keys, values, log_decay, flops=rows * width * W * 2,
    )
    got = lax.all_to_all(pay, "ctx", 0, 0, tiled=True)
    probs, mask, within = call(
        inside,
        [shape(heads, span, span), shape(heads, span, span, dtype=F32), shape(rows, width, dtype=F32)],
        queries, keys, values, col, row, flops=rows * width * span * 4,
    )
    (grad_norm,) = call(
        grad_of_norm, [shape(rows, width, dtype=F32)], core, out_grad, other_grad, out_weight,
        flops=2 * rows * width * model, smem=1,
    )
    sent, high, low = call(
        forward_scan, [shape(count, slots), shape(count, count), shape(count, count)], got,
        flops=4 * count * count * slots,
    )
    state = lax.all_to_all(sent, "ctx", 0, 0, tiled=True)
    normed, grad_att, pay = call(
        norm_and_grad,
        [shape(rows, width), shape(rows, width), shape(count, slots)],
        queries, state, col, within, grad_norm, flops=rows * width * W * 4,
    )
    got = lax.all_to_all(pay, "ctx", 0, 0, tiled=True)
    own, other = call(
        mix, [shape(rows, model // 2, dtype=F32), shape(rows, model // 2)], core, normed, out_weight,
        flops=2 * rows * width * model, smem=1,
    )
    theirs = lax.ppermute(other, "head", swap)
    grad_q, gk_part, gv_part = call(
        score_grads,
        [shape(rows, width), shape(rows, width, dtype=F32), shape(rows, width, dtype=F32)],
        queries, keys, values, grad_att, state, col, probs, mask, flops=rows * width * span * 9,
    )
    (sent,) = call(backward_scan, [shape(count, slots)], got, high, low, flops=4 * count * count * slots)
    leaving = lax.all_to_all(sent, "ctx", 0, 0, tiled=True)
    mixed = (own + theirs.astype(F32)).astype(BF)
    grad_k, grad_v = call(
        finish, [shape(rows, width), shape(rows, width)], keys, values, leaving, col, gk_part, gv_part,
        flops=rows * width * W * 4,
    )
    return mixed, grad_q, grad_k, grad_v


def solution(mesh):
    split = P("ctx", "head")
    return jax.shard_map(
        local,
        mesh=mesh,
        in_specs=(split, split, split, P("head", "ctx"), P("head", None), split),
        out_specs=(split,) * 4,
        check_vma=False,
    )
```

```python
import functools

import jax
import jax.numpy as jnp
from jax import lax
from jax.experimental import pallas as pl
from jax.experimental.pallas import tpu as pltpu
from jax.sharding import PartitionSpec as P

EPS = 1e-05
F32 = jnp.float32
BF = jnp.bfloat16
W = 128
OWN = 4


def dot(a, b, da=1, db=0, precision=None):
    return lax.dot_general(
        a, b, (((da,), (db,)), ((), ())), preferred_element_type=F32, precision=precision
    )


def call(body, outs, *args, flops=0, smem=0, scratch=()):
    spec = [pl.BlockSpec(memory_space=pltpu.SMEM)] * smem
    spec += [pl.BlockSpec(memory_space=pltpu.VMEM)] * (len(args) - smem)
    moved = sum(a.size * a.dtype.itemsize for a in (*args, *outs))
    return pl.pallas_call(
        body,
        out_shape=outs,
        in_specs=spec,
        out_specs=[pl.BlockSpec(memory_space=pltpu.VMEM)] * len(outs),
        scratch_shapes=[pltpu.VMEM(dims, F32) for dims in scratch],
        compiler_params=pltpu.CompilerParams(vmem_limit_bytes=12 << 20),
        cost_estimate=pl.CostEstimate(flops=flops, bytes_accessed=moved, transcendentals=0),
        name=body.__name__ if hasattr(body, "__name__") else body.func.__name__,
    )(*args)


def shape(*dims, dtype=BF):
    return jax.ShapeDtypeStruct(dims, dtype)


def head_cols(h):
    return slice(h * W, (h + 1) * W)


def block_delta(k_ref, v_ref, ld_ref, pay_ref, col_ref, row_ref, delta_ref, mixed_ref):
    heads, span = ld_ref.shape
    slots, six = delta_ref.shape[0] // OWN, OWN + 2
    per = slots // heads
    ld = ld_ref[...]
    a = lax.broadcasted_iota(jnp.int32, (span, span), 0)
    b = lax.broadcasted_iota(jnp.int32, (span, span), 1)
    col = dot((b <= a).astype(F32), ld, 1, 1, precision=lax.Precision.HIGHEST)
    last = col[span - 1 : span, :]
    weight = jnp.exp(last - col)
    lane = lax.broadcasted_iota(jnp.int32, (per, W), 1)
    for h in range(heads):
        kw = (k_ref[:, head_cols(h)].astype(F32) * weight[:, h : h + 1]).astype(BF)
        delta_ref[h * W : (h + 1) * W] = dot(kw, v_ref[:, head_cols(h)], 0, 0)
        end = jnp.broadcast_to(last[:, h : h + 1], (per, W))
        hi = end.astype(BF).astype(F32)
        mid = (end - hi).astype(BF).astype(F32)
        low = end - hi - mid
        tail = jnp.where(lane == 0, hi, jnp.where(lane == 1, mid, jnp.where(lane == 2, low, 0.0)))
        mixed_ref[pl.ds(h * per * six + OWN, per, stride=six)] = tail
        mixed_ref[pl.ds(h * per * six + OWN + 1, per, stride=six)] = tail
    for r in range(OWN):
        mixed_ref[pl.ds(r, slots, stride=six)] = delta_ref[pl.ds(r, slots, stride=OWN)]
    pay_ref[...] = mixed_ref[...].astype(BF)
    col_ref[0] = jnp.exp(col)
    col_ref[1] = weight
    col_ref[2] = col
    row_ref[...] = dot(ld, (a <= b).astype(F32), precision=lax.Precision.HIGHEST)


def inside(q_ref, k_ref, v_ref, col_ref, row_ref, probs_ref, mask_ref, in_ref):
    heads, span = row_ref.shape
    a = lax.broadcasted_iota(jnp.int32, (span, span), 0)
    b = lax.broadcasted_iota(jnp.int32, (span, span), 1)
    for h in range(heads):
        gap = col_ref[2][:, h : h + 1] - row_ref[h : h + 1, :]
        mask = jnp.where(b <= a, jnp.exp(jnp.minimum(gap, 0.0)), 0.0)
        mask_ref[h] = mask
        probs = (dot(q_ref[:, head_cols(h)], k_ref[:, head_cols(h)], 1, 1) * mask).astype(BF)
        probs_ref[h] = probs
        in_ref[:, head_cols(h)] = dot(probs, v_ref[:, head_cols(h)])


def grad_of_norm(core_ref, own_ref, other_ref, w_ref, out_ref):
    width = own_ref.shape[1]
    mine = pl.multiple_of(core_ref[0] * width, width)
    theirs = pl.multiple_of((1 - core_ref[0]) * width, width)
    out_ref[...] = dot(own_ref[...], w_ref[:, pl.ds(mine, width)], 1, 1) + dot(
        other_ref[...], w_ref[:, pl.ds(theirs, width)], 1, 1
    )


def forward_scan(x_ref, y_ref, mh_ref, ml_ref, x32_ref, y32_ref):
    count = mh_ref.shape[0]
    six = x_ref.shape[0] // count
    x32_ref[...] = x_ref[...].astype(F32)
    i = lax.broadcasted_iota(jnp.int32, (count, count), 0)
    j = lax.broadcasted_iota(jnp.int32, (count, count), 1)
    before = (j < i).astype(BF)
    gap = jnp.zeros((count, count), F32)
    ends = x32_ref[pl.ds(OWN, count, stride=six)]
    for piece in range(3):
        gap = gap + dot(before, jnp.where(j < i, ends[:, piece : piece + 1], 0.0).astype(BF))
    reach = jnp.where(j < i, jnp.exp(jnp.minimum(gap, 0.0)), 0.0)
    high = reach.astype(BF)
    low = (reach - high.astype(F32)).astype(BF)
    mh_ref[...] = high
    ml_ref[...] = low
    for r in range(OWN):
        x = x32_ref[pl.ds(r, count, stride=six)].astype(BF)
        y32_ref[pl.ds(r, count, stride=OWN)] = dot(high, x) + dot(low, x)
    y_ref[...] = y32_ref[...].astype(BF)


def backward_scan(x_ref, mh_ref, ml_ref, y_ref, x32_ref, y32_ref):
    count = mh_ref.shape[0]
    x32_ref[...] = x_ref[...].astype(F32)
    for r in range(OWN):
        x = x32_ref[pl.ds(r, count, stride=OWN)].astype(BF)
        y32_ref[pl.ds(r, count, stride=OWN)] = dot(mh_ref[...], x, 0, 0) + dot(ml_ref[...], x, 0, 0)
    y_ref[...] = y32_ref[...].astype(BF)


def norm_and_grad(q_ref, s_ref, col_ref, in_ref, gn_ref, normed_ref, g_ref, pay_ref):
    heads = in_ref.shape[1] // W
    for h in range(heads):
        cols = head_cols(h)
        growth = col_ref[0][:, h : h + 1]
        q = q_ref[:, cols]
        att = in_ref[:, cols] + growth * dot(q, s_ref[h * W : (h + 1) * W])
        inv = lax.rsqrt(jnp.mean(att * att, axis=1, keepdims=True) + EPS)
        normed_ref[:, cols] = (att * inv).astype(BF)
        gn = gn_ref[:, cols]
        g = inv * gn - att * (inv * inv * inv * jnp.mean(gn * att, axis=1, keepdims=True))
        g = g.astype(BF)
        g_ref[:, cols] = g
        pay_ref[h * W : (h + 1) * W] = dot((q.astype(F32) * growth).astype(BF), g, 0, 0).astype(BF)


def mix(core_ref, normed_ref, w_ref, own_ref, other_ref):
    width = own_ref.shape[1]
    mine = pl.multiple_of(core_ref[0] * width, width)
    theirs = pl.multiple_of((1 - core_ref[0]) * width, width)
    other_ref[...] = dot(normed_ref[...], w_ref[:, pl.ds(theirs, width)]).astype(BF)
    own_ref[...] = dot(normed_ref[...], w_ref[:, pl.ds(mine, width)])


def score_grads(q_ref, k_ref, v_ref, g_ref, s_ref, col_ref, probs_ref, mask_ref, gq_ref, gk_ref, gv_ref):
    heads = probs_ref.shape[0]
    for h in range(heads):
        cols = head_cols(h)
        g = g_ref[:, cols]
        d = (dot(g, v_ref[:, cols], 1, 1) * mask_ref[h]).astype(BF)
        carried = dot(g, s_ref[h * W : (h + 1) * W], 1, 1)
        gq_ref[:, cols] = (dot(d, k_ref[:, cols]) + col_ref[0][:, h : h + 1] * carried).astype(BF)
        gk_ref[:, cols] = dot(d, q_ref[:, cols], 0, 0)
        gv_ref[:, cols] = dot(probs_ref[h], g, 0, 0)


def finish(k_ref, v_ref, e_ref, col_ref, gkp_ref, gvp_ref, gk_ref, gv_ref):
    heads = gk_ref.shape[1] // W
    for h in range(heads):
        cols = head_cols(h)
        weight = col_ref[1][:, h : h + 1]
        e = e_ref[h * W : (h + 1) * W]
        gk_ref[:, cols] = (gkp_ref[:, cols] + weight * dot(v_ref[:, cols], e, 1, 1)).astype(BF)
        gv_ref[:, cols] = (gvp_ref[:, cols] + weight * dot(k_ref[:, cols], e)).astype(BF)


def local(queries, keys, values, log_decay, out_weight, out_grad):
    rows, width = queries.shape
    heads, span = log_decay.shape
    count = lax.axis_size("ctx")
    lines = heads * W
    assert lines == OWN * count
    model = out_weight.shape[1]
    core = lax.axis_index("head").astype(jnp.int32).reshape(1)
    swap = [(0, 1), (1, 0)]

    other_grad = lax.ppermute(out_grad, "head", swap)
    pay, col, row = call(
        block_delta,
        [shape(count * (OWN + 2), W), shape(3, rows, heads, dtype=F32), shape(heads, span, dtype=F32)],
        keys, values, log_decay, flops=rows * width * W * 2,
        scratch=[(lines, W), (count * (OWN + 2), W)],
    )
    got = lax.all_to_all(pay.reshape(-1, 2, W), "ctx", 0, 0, tiled=True).reshape(-1, W)
    probs, mask, within = call(
        inside,
        [shape(heads, span, span), shape(heads, span, span, dtype=F32), shape(rows, width, dtype=F32)],
        queries, keys, values, col, row, flops=rows * width * span * 4,
    )
    (grad_norm,) = call(
        grad_of_norm, [shape(rows, width, dtype=F32)], core, out_grad, other_grad, out_weight,
        flops=2 * rows * width * model, smem=1,
    )
    sent, high, low = call(
        forward_scan, [shape(lines, W), shape(count, count), shape(count, count)], got,
        flops=4 * count * lines * W, scratch=[(count * (OWN + 2), W), (lines, W)],
    )
    state = lax.all_to_all(sent, "ctx", 0, 0, tiled=True)
    normed, grad_att, pay = call(
        norm_and_grad,
        [shape(rows, width), shape(rows, width), shape(lines, W)],
        queries, state, col, within, grad_norm, flops=rows * width * W * 4,
    )
    got = lax.all_to_all(pay, "ctx", 0, 0, tiled=True)
    own, other = call(
        mix, [shape(rows, model // 2, dtype=F32), shape(rows, model // 2)], core, normed, out_weight,
        flops=2 * rows * width * model, smem=1,
    )
    theirs = lax.ppermute(other, "head", swap)
    grad_q, gk_part, gv_part = call(
        score_grads,
        [shape(rows, width), shape(rows, width, dtype=F32), shape(rows, width, dtype=F32)],
        queries, keys, values, grad_att, state, col, probs, mask, flops=rows * width * span * 9,
    )
    (sent,) = call(
        backward_scan, [shape(lines, W)], got, high, low, flops=4 * count * lines * W,
        scratch=[(lines, W), (lines, W)],
    )
    leaving = lax.all_to_all(sent, "ctx", 0, 0, tiled=True)
    mixed = (own + theirs.astype(F32)).astype(BF)
    mixed, gk_part = lax.optimization_barrier((mixed, gk_part))
    grad_k, grad_v = call(
        finish, [shape(rows, width), shape(rows, width)], keys, values, leaving, col, gk_part, gv_part,
        flops=rows * width * W * 4,
    )
    return mixed, grad_q, grad_k, grad_v


def solution(mesh):
    split = P("ctx", "head")
    return jax.shard_map(
        local,
        mesh=mesh,
        in_specs=(split, split, split, P("head", "ctx"), P("head", None), split),
        out_specs=(split,) * 4,
        check_vma=False,
    )
```

```python
import math

import jax
import jax.numpy as jnp
from jax import lax
from jax.experimental import pallas as pl
from jax.experimental.pallas import tpu as pltpu
from jax.sharding import PartitionSpec as P

EPS = 1e-05
F32 = jnp.float32
BF = jnp.bfloat16
W = 128
OWN = 4
EXACT = lax.Precision.HIGHEST


def dot(a, b, da=1, db=0, precision=None):
    return lax.dot_general(
        a, b, (((da,), (db,)), ((), ())), preferred_element_type=F32, precision=precision
    )


def call(body, outs, *args, flops=0, far=(), smem=0, scratch=()):
    def spec(i):
        if i < smem:
            return pl.BlockSpec(memory_space=pltpu.SMEM)
        return pl.BlockSpec(memory_space=pltpu.HBM if i in far else pltpu.VMEM)

    buffers = [pltpu.VMEM(dims, kind) for dims, kind in scratch]
    buffers += [pltpu.VMEM(args[i].shape, args[i].dtype) for i in far]
    if far:
        buffers += [pltpu.SemaphoreType.DMA((len(far),))]
    args = [pltpu.with_memory_space_constraint(a, pltpu.HBM) if i in far else a for i, a in enumerate(args)]
    moved = sum(math.prod(a.shape) * a.dtype.itemsize for a in (*args, *outs))
    return pl.pallas_call(
        body,
        out_shape=outs,
        in_specs=[spec(i) for i in range(len(args))],
        out_specs=[pl.BlockSpec(memory_space=pltpu.VMEM)] * len(outs),
        scratch_shapes=buffers,
        compiler_params=pltpu.CompilerParams(vmem_limit_bytes=12 << 20),
        cost_estimate=pl.CostEstimate(flops=flops, bytes_accessed=moved, transcendentals=0),
        name=body.__name__,
    )(*args)


def fetch(sources, places, sems):
    copies = [pltpu.make_async_copy(a, b, sems.at[i]) for i, (a, b) in enumerate(zip(sources, places))]
    for copy in copies:
        copy.start()
    return copies


def shape(*dims, dtype=BF):
    return jax.ShapeDtypeStruct(dims, dtype)


def near(*dims, dtype=BF):
    return pltpu.VMEM(dims, dtype)


def head_cols(h):
    return slice(h * W, (h + 1) * W)


def head_rows(h):
    return slice(h * W, (h + 1) * W)


def grid_of(n):
    return lax.broadcasted_iota(jnp.int32, (n, n), 0), lax.broadcasted_iota(jnp.int32, (n, n), 1)


def block_delta(k_far, v_far, ld_far, pay_ref, col_ref, delta_ref, mixed_ref, k_ref, v_ref, ld_ref, sems):
    heads, span = ld_ref.shape
    slots, six = delta_ref.shape[0] // OWN, OWN + 2
    per = slots // heads
    copies = fetch((k_far, v_far, ld_far), (k_ref, v_ref, ld_ref), sems)
    a, b = grid_of(span)
    lane = lax.broadcasted_iota(jnp.int32, (per, W), 1)
    copies[2].wait()
    col = dot((b <= a).astype(F32), ld_ref[...], 1, 1, precision=EXACT)
    last = col[span - 1 : span, :]
    weight = jnp.exp(last - col)
    copies[0].wait()
    copies[1].wait()
    for h in range(heads):
        kw = (k_ref[:, head_cols(h)].astype(F32) * weight[:, h : h + 1]).astype(BF)
        delta_ref[head_rows(h)] = dot(kw, v_ref[:, head_cols(h)], 0, 0)
        end = jnp.broadcast_to(last[:, h : h + 1], (per, W))
        hi = end.astype(BF).astype(F32)
        mid = (end - hi).astype(BF).astype(F32)
        low = end - hi - mid
        tail = jnp.where(lane == 0, hi, jnp.where(lane == 1, mid, jnp.where(lane == 2, low, 0.0)))
        mixed_ref[pl.ds(h * per * six + OWN, per, stride=six)] = tail
        mixed_ref[pl.ds(h * per * six + OWN + 1, per, stride=six)] = tail
    for r in range(OWN):
        mixed_ref[pl.ds(r, slots, stride=six)] = delta_ref[pl.ds(r, slots, stride=OWN)]
    pay_ref[...] = mixed_ref[...].astype(BF)
    col_ref[:, :heads] = jnp.exp(col)
    col_ref[:, heads : 2 * heads] = weight
    col_ref[:, 2 * heads : 3 * heads] = col


def masked_probs(h, heads, q, k, col_ref, row, a, b):
    gap = col_ref[:, 2 * heads + h : 2 * heads + h + 1] - row[h : h + 1, :]
    mask = jnp.where(b <= a, jnp.exp(jnp.minimum(gap, 0.0)), 0.0)
    return (dot(q, k, 1, 1) * mask).astype(BF), mask


def before_norm(core_ref, q_ref, col_ref, ld_ref, other_ref, k_far, v_far, own_far, w_far, in_ref, gn_ref, k_ref, v_ref, own_ref, w_ref, sems):
    heads, span = ld_ref.shape
    copies = fetch((k_far, v_far, own_far, w_far), (k_ref, v_ref, own_ref, w_ref), sems)
    a, b = grid_of(span)
    row = dot(ld_ref[...], (a <= b).astype(F32), precision=EXACT)
    copies[0].wait()
    copies[1].wait()
    for h in range(heads):
        cols = head_cols(h)
        probs, _ = masked_probs(h, heads, q_ref[:, cols], k_ref[:, cols], col_ref, row, a, b)
        in_ref[:, cols] = dot(probs, v_ref[:, cols])
    width = own_ref.shape[1]
    mine = pl.multiple_of(core_ref[0] * width, width)
    theirs = pl.multiple_of((1 - core_ref[0]) * width, width)
    for copy in copies[2:]:
        copy.wait()
    gn_ref[...] = dot(own_ref[...], w_ref[:, pl.ds(mine, width)], 1, 1) + dot(
        other_ref[...], w_ref[:, pl.ds(theirs, width)], 1, 1
    )


def forward_scan(x_ref, y_ref, reach_ref, x32_ref, y32_ref):
    count = reach_ref.shape[1]
    six = x_ref.shape[0] // count
    x32_ref[...] = x_ref[...].astype(F32)
    i, j = grid_of(count)
    before = (j < i).astype(BF)
    gap = jnp.zeros((count, count), F32)
    ends = x32_ref[pl.ds(OWN, count, stride=six)]
    for piece in range(3):
        gap = gap + dot(before, jnp.where(j < i, ends[:, piece : piece + 1], 0.0).astype(BF))
    reach = jnp.where(j < i, jnp.exp(jnp.minimum(gap, 0.0)), 0.0)
    high = reach.astype(BF)
    low = (reach - high.astype(F32)).astype(BF)
    reach_ref[:count] = high
    reach_ref[count:] = low
    for r in range(OWN):
        x = x32_ref[pl.ds(r, count, stride=six)].astype(BF)
        y32_ref[pl.ds(r, count, stride=OWN)] = dot(high, x) + dot(low, x)
    y_ref[...] = y32_ref[...].astype(BF)


def backward_scan(x_ref, reach_ref, y_ref, x32_ref, y32_ref):
    count = reach_ref.shape[1]
    x32_ref[...] = x_ref[...].astype(F32)
    high, low = reach_ref[:count], reach_ref[count:]
    for r in range(OWN):
        x = x32_ref[pl.ds(r, count, stride=OWN)].astype(BF)
        y32_ref[pl.ds(r, count, stride=OWN)] = dot(high, x, 0, 0) + dot(low, x, 0, 0)
    y_ref[...] = y32_ref[...].astype(BF)


def norm_and_grad(q_ref, s_ref, col_ref, in_ref, gn_ref, normed_ref, g_ref, pay_ref):
    heads = in_ref.shape[1] // W
    for h in range(heads):
        cols = head_cols(h)
        growth = col_ref[:, h : h + 1]
        q = q_ref[:, cols]
        att = in_ref[:, cols] + growth * dot(q, s_ref[head_rows(h)])
        inv = lax.rsqrt(jnp.mean(att * att, axis=1, keepdims=True) + EPS)
        normed_ref[:, cols] = (att * inv).astype(BF)
        gn = gn_ref[:, cols]
        g = inv * gn - att * (inv * inv * inv * jnp.mean(gn * att, axis=1, keepdims=True))
        g = g.astype(BF)
        g_ref[:, cols] = g
        pay_ref[head_rows(h)] = dot((q.astype(F32) * growth).astype(BF), g, 0, 0).astype(BF)


def mix(core_ref, normed_ref, other_ref, w_far, w_other_far, out_ref, w_ref, w_other_ref, sems):
    width = out_ref.shape[1]
    mine = pl.multiple_of(core_ref[0] * width, width)
    copies = fetch(
        (w_far.at[:, pl.ds(mine, width)], w_other_far.at[:, pl.ds(mine, width)]),
        (w_ref.at[:, pl.ds(0, width)], w_other_ref.at[:, pl.ds(0, width)]),
        sems,
    )
    copies[0].wait()
    copies[1].wait()
    out_ref[...] = (
        dot(normed_ref[...], w_ref[:, :width]) + dot(other_ref[...], w_other_ref[:, :width])
    ).astype(BF)


def after_norm(g_ref, s_ref, col_ref, ld_ref, q_far, k_far, v_far, gq_ref, gk_ref, gv_ref, q_ref, k_ref, v_ref, sems):
    heads, span = ld_ref.shape
    copies = fetch((q_far, k_far, v_far), (q_ref, k_ref, v_ref), sems)
    a, b = grid_of(span)
    row = dot(ld_ref[...], (a <= b).astype(F32), precision=EXACT)
    for copy in copies:
        copy.wait()
    for h in range(heads):
        cols = head_cols(h)
        q, k, g = q_ref[:, cols], k_ref[:, cols], g_ref[:, cols]
        probs, mask = masked_probs(h, heads, q, k, col_ref, row, a, b)
        d = (dot(g, v_ref[:, cols], 1, 1) * mask).astype(BF)
        carried = dot(g, s_ref[head_rows(h)], 1, 1)
        gq_ref[:, cols] = (dot(d, k) + col_ref[:, h : h + 1] * carried).astype(BF)
        gk_ref[:, cols] = dot(d, q, 0, 0)
        gv_ref[:, cols] = dot(probs, g, 0, 0)


def finish(k_ref, v_ref, e_ref, col_ref, gkp_ref, gvp_ref, gk_ref, gv_ref):
    heads = gk_ref.shape[1] // W
    for h in range(heads):
        cols = head_cols(h)
        weight = col_ref[:, heads + h : heads + h + 1]
        e = e_ref[head_rows(h)]
        gk_ref[:, cols] = (gkp_ref[:, cols] + weight * dot(v_ref[:, cols], e, 1, 1)).astype(BF)
        gv_ref[:, cols] = (gvp_ref[:, cols] + weight * dot(k_ref[:, cols], e)).astype(BF)


def local(queries, keys, values, log_decay, out_weight, out_grad):
    rows, width = queries.shape
    heads, span = log_decay.shape
    count = lax.axis_size("ctx")
    lines = heads * W
    assert lines == OWN * count and rows == span and span >= W
    model = out_weight.shape[1]
    core = lax.axis_index("head").astype(jnp.int32).reshape(1)
    swap = [(0, 1), (1, 0)]
    exchange = count * (OWN + 2)

    pay, col = call(
        block_delta, [near(exchange, W), near(rows, W, dtype=F32)], keys, values, log_decay,
        flops=rows * width * W * 2, far=(0, 1, 2), scratch=[((lines, W), F32), ((exchange, W), F32)],
    )
    got = lax.all_to_all(pay.reshape(-1, 2, W), "ctx", 0, 0, tiled=True).reshape(-1, W)
    other_grad = lax.ppermute(out_grad, "head", swap)
    other_weight = lax.ppermute(out_weight, "head", swap)
    within, grad_norm = call(
        before_norm, [near(rows, width, dtype=F32), near(rows, width, dtype=F32)],
        core, queries, col, log_decay, other_grad, keys, values, out_grad, out_weight,
        flops=rows * width * (span * 4 + model * 2), smem=1, far=(5, 6, 7, 8),
    )
    sent, reach = call(
        forward_scan, [near(lines, W), near(2 * count, count)], got,
        flops=4 * count * lines * W, scratch=[((exchange, W), F32), ((lines, W), F32)],
    )
    state = lax.all_to_all(sent, "ctx", 0, 0, tiled=True)
    normed, grad_att, pay = call(
        norm_and_grad, [shape(rows, width), near(rows, width), near(lines, W)],
        queries, state, col, within, grad_norm, flops=rows * width * W * 4,
    )
    got = lax.all_to_all(pay, "ctx", 0, 0, tiled=True)
    other_normed = lax.ppermute(normed, "head", swap)
    grad_q, gk_part, gv_part = call(
        after_norm,
        [shape(rows, width), near(rows, width, dtype=F32), near(rows, width, dtype=F32)],
        grad_att, state, col, log_decay, queries, keys, values, flops=rows * width * span * 9, far=(4, 5, 6),
    )
    (sent,) = call(
        backward_scan, [near(lines, W)], got, reach, flops=4 * count * lines * W,
        scratch=[((lines, W), F32), ((lines, W), F32)],
    )
    leaving = lax.all_to_all(sent, "ctx", 0, 0, tiled=True)
    (mixed,) = call(
        mix, [shape(rows, model // 2)], core, normed, other_normed, out_weight, other_weight,
        flops=2 * rows * width * model, smem=1, far=(3, 4),
    )
    mixed, gk_part = lax.optimization_barrier((mixed, gk_part))
    grad_k, grad_v = call(
        finish, [shape(rows, width), shape(rows, width)], keys, values, leaving, col, gk_part, gv_part,
        flops=rows * width * W * 4,
    )
    return mixed, grad_q, grad_k, grad_v


def solution(mesh):
    split = P("ctx", "head")
    return jax.shard_map(
        local,
        mesh=mesh,
        in_specs=(split, split, split, P("head", "ctx"), P("head", None), split),
        out_specs=(split,) * 4,
        check_vma=False,
    )
```

```python
import math

import jax
import jax.numpy as jnp
from jax import lax
from jax.experimental import pallas as pl
from jax.experimental.pallas import tpu as pltpu
from jax.sharding import PartitionSpec as P

EPS = 1e-05
F32 = jnp.float32
BF = jnp.bfloat16
W = 128
OWN = 4
EXACT = lax.Precision.HIGHEST


def dot(a, b, da=1, db=0, precision=None):
    return lax.dot_general(
        a, b, (((da,), (db,)), ((), ())), preferred_element_type=F32, precision=precision
    )


def call(body, outs, *args, flops=0, far=(), smem=0, scratch=()):
    def spec(i):
        if i < smem:
            return pl.BlockSpec(memory_space=pltpu.SMEM)
        return pl.BlockSpec(memory_space=pltpu.HBM if i in far else pltpu.VMEM)

    buffers = [pltpu.VMEM(dims, kind) for dims, kind in scratch]
    buffers += [pltpu.VMEM(args[i].shape, args[i].dtype) for i in far]
    if far:
        buffers += [pltpu.SemaphoreType.DMA((len(far),))]
    args = [pltpu.with_memory_space_constraint(a, pltpu.HBM) if i in far else a for i, a in enumerate(args)]
    moved = sum(math.prod(a.shape) * a.dtype.itemsize for a in (*args, *outs))
    return pl.pallas_call(
        body,
        out_shape=outs,
        in_specs=[spec(i) for i in range(len(args))],
        out_specs=[pl.BlockSpec(memory_space=pltpu.VMEM)] * len(outs),
        scratch_shapes=buffers,
        compiler_params=pltpu.CompilerParams(vmem_limit_bytes=12 << 20),
        cost_estimate=pl.CostEstimate(flops=flops, bytes_accessed=moved, transcendentals=0),
        name=body.__name__,
    )(*args)


def fetch(sources, places, sems):
    copies = [pltpu.make_async_copy(a, b, sems.at[i]) for i, (a, b) in enumerate(zip(sources, places))]
    for copy in copies:
        copy.start()
    return copies


def shape(*dims, dtype=BF):
    return jax.ShapeDtypeStruct(dims, dtype)


def near(*dims, dtype=BF):
    return pltpu.VMEM(dims, dtype)


def head_cols(h):
    return slice(h * W, (h + 1) * W)


def head_rows(h):
    return slice(h * W, (h + 1) * W)


def grid_of(n):
    return lax.broadcasted_iota(jnp.int32, (n, n), 0), lax.broadcasted_iota(jnp.int32, (n, n), 1)


def block_delta(k_far, v_far, ld_far, pay_ref, col_ref, delta_ref, mixed_ref, k_ref, v_ref, ld_ref, sems):
    heads, span = ld_ref.shape
    slots, six = delta_ref.shape[0] // OWN, OWN + 2
    per = slots // heads
    copies = fetch((k_far, v_far, ld_far), (k_ref, v_ref, ld_ref), sems)
    a, b = grid_of(span)
    lane = lax.broadcasted_iota(jnp.int32, (per, W), 1)
    copies[2].wait()
    col = dot((b <= a).astype(F32), ld_ref[...], 1, 1, precision=EXACT)
    last = col[span - 1 : span, :]
    weight = jnp.exp(last - col)
    copies[0].wait()
    copies[1].wait()
    for h in range(heads):
        kw = (k_ref[:, head_cols(h)].astype(F32) * weight[:, h : h + 1]).astype(BF)
        delta_ref[head_rows(h)] = dot(kw, v_ref[:, head_cols(h)], 0, 0)
        end = jnp.broadcast_to(last[:, h : h + 1], (per, W))
        hi = end.astype(BF).astype(F32)
        mid = (end - hi).astype(BF).astype(F32)
        low = end - hi - mid
        tail = jnp.where(lane == 0, hi, jnp.where(lane == 1, mid, jnp.where(lane == 2, low, 0.0)))
        mixed_ref[pl.ds(h * per * six + OWN, per, stride=six)] = tail
        mixed_ref[pl.ds(h * per * six + OWN + 1, per, stride=six)] = tail
    for r in range(OWN):
        mixed_ref[pl.ds(r, slots, stride=six)] = delta_ref[pl.ds(r, slots, stride=OWN)]
    pay_ref[...] = mixed_ref[...].astype(BF)
    col_ref[:, :heads] = jnp.exp(col)
    col_ref[:, heads : 2 * heads] = weight
    col_ref[:, 2 * heads : 3 * heads] = col


def masked_probs(h, heads, q, k, col_ref, row, a, b):
    gap = col_ref[:, 2 * heads + h : 2 * heads + h + 1] - row[h : h + 1, :]
    mask = jnp.where(b <= a, jnp.exp(jnp.minimum(gap, 0.0)), 0.0)
    return (dot(q, k, 1, 1) * mask).astype(BF), mask


def before_norm(core_ref, col_ref, other_ref, ld_far, q_far, k_far, v_far, own_far, w_far, in_ref, gn_ref, ld_ref, q_ref, k_ref, v_ref, own_ref, w_ref, sems):
    heads, span = ld_ref.shape
    copies = fetch((ld_far, q_far, k_far, v_far, own_far, w_far), (ld_ref, q_ref, k_ref, v_ref, own_ref, w_ref), sems)
    a, b = grid_of(span)
    copies[0].wait()
    row = dot(ld_ref[...], (a <= b).astype(F32), precision=EXACT)
    for copy in copies[1:4]:
        copy.wait()
    for h in range(heads):
        cols = head_cols(h)
        probs, _ = masked_probs(h, heads, q_ref[:, cols], k_ref[:, cols], col_ref, row, a, b)
        in_ref[:, cols] = dot(probs, v_ref[:, cols])
    width = own_ref.shape[1]
    mine = pl.multiple_of(core_ref[0] * width, width)
    theirs = pl.multiple_of((1 - core_ref[0]) * width, width)
    for copy in copies[4:]:
        copy.wait()
    gn_ref[...] = dot(own_ref[...], w_ref[:, pl.ds(mine, width)], 1, 1) + dot(
        other_ref[...], w_ref[:, pl.ds(theirs, width)], 1, 1
    )


def forward_scan(x_ref, y_ref, reach_ref, x32_ref, y32_ref):
    count = reach_ref.shape[1]
    six = x_ref.shape[0] // count
    x32_ref[...] = x_ref[...].astype(F32)
    i, j = grid_of(count)
    before = (j < i).astype(BF)
    gap = jnp.zeros((count, count), F32)
    ends = x32_ref[pl.ds(OWN, count, stride=six)]
    for piece in range(3):
        gap = gap + dot(before, jnp.where(j < i, ends[:, piece : piece + 1], 0.0).astype(BF))
    reach = jnp.where(j < i, jnp.exp(jnp.minimum(gap, 0.0)), 0.0)
    high = reach.astype(BF)
    low = (reach - high.astype(F32)).astype(BF)
    reach_ref[:count] = high
    reach_ref[count:] = low
    for r in range(OWN):
        x = x32_ref[pl.ds(r, count, stride=six)].astype(BF)
        y32_ref[pl.ds(r, count, stride=OWN)] = dot(high, x) + dot(low, x)
    y_ref[...] = y32_ref[...].astype(BF)


def backward_scan(x_ref, reach_ref, y_ref, x32_ref, y32_ref):
    count = reach_ref.shape[1]
    x32_ref[...] = x_ref[...].astype(F32)
    high, low = reach_ref[:count], reach_ref[count:]
    for r in range(OWN):
        x = x32_ref[pl.ds(r, count, stride=OWN)].astype(BF)
        y32_ref[pl.ds(r, count, stride=OWN)] = dot(high, x, 0, 0) + dot(low, x, 0, 0)
    y_ref[...] = y32_ref[...].astype(BF)


def norm_and_grad(q_ref, s_ref, col_ref, in_ref, gn_ref, normed_ref, g_ref, pay_ref):
    heads = in_ref.shape[1] // W
    for h in range(heads):
        cols = head_cols(h)
        growth = col_ref[:, h : h + 1]
        q = q_ref[:, cols]
        att = in_ref[:, cols] + growth * dot(q, s_ref[head_rows(h)])
        inv = lax.rsqrt(jnp.mean(att * att, axis=1, keepdims=True) + EPS)
        normed_ref[:, cols] = (att * inv).astype(BF)
        gn = gn_ref[:, cols]
        g = inv * gn - att * (inv * inv * inv * jnp.mean(gn * att, axis=1, keepdims=True))
        g = g.astype(BF)
        g_ref[:, cols] = g
        pay_ref[head_rows(h)] = dot((q.astype(F32) * growth).astype(BF), g, 0, 0).astype(BF)


def mix(core_ref, normed_ref, other_ref, w_far, w_other_far, out_ref, w_ref, w_other_ref, sems):
    width = out_ref.shape[1]
    mine = pl.multiple_of(core_ref[0] * width, width)
    copies = fetch(
        (w_far.at[:, pl.ds(mine, width)], w_other_far.at[:, pl.ds(mine, width)]),
        (w_ref.at[:, pl.ds(0, width)], w_other_ref.at[:, pl.ds(0, width)]),
        sems,
    )
    copies[0].wait()
    copies[1].wait()
    out_ref[...] = (
        dot(normed_ref[...], w_ref[:, :width]) + dot(other_ref[...], w_other_ref[:, :width])
    ).astype(BF)


def after_norm(g_ref, s_ref, col_ref, ld_far, q_far, k_far, v_far, gq_ref, gk_ref, gv_ref, ld_ref, q_ref, k_ref, v_ref, sems):
    heads, span = ld_ref.shape
    copies = fetch((ld_far, q_far, k_far, v_far), (ld_ref, q_ref, k_ref, v_ref), sems)
    a, b = grid_of(span)
    copies[0].wait()
    row = dot(ld_ref[...], (a <= b).astype(F32), precision=EXACT)
    for copy in copies[1:]:
        copy.wait()
    for h in range(heads):
        cols = head_cols(h)
        q, k, g = q_ref[:, cols], k_ref[:, cols], g_ref[:, cols]
        probs, mask = masked_probs(h, heads, q, k, col_ref, row, a, b)
        d = (dot(g, v_ref[:, cols], 1, 1) * mask).astype(BF)
        carried = dot(g, s_ref[head_rows(h)], 1, 1)
        gq_ref[:, cols] = (dot(d, k) + col_ref[:, h : h + 1] * carried).astype(BF)
        gk_ref[:, cols] = dot(d, q, 0, 0)
        gv_ref[:, cols] = dot(probs, g, 0, 0)


def finish(k_ref, v_ref, e_ref, col_ref, gkp_ref, gvp_ref, gk_ref, gv_ref):
    heads = gk_ref.shape[1] // W
    for h in range(heads):
        cols = head_cols(h)
        weight = col_ref[:, heads + h : heads + h + 1]
        e = e_ref[head_rows(h)]
        gk_ref[:, cols] = (gkp_ref[:, cols] + weight * dot(v_ref[:, cols], e, 1, 1)).astype(BF)
        gv_ref[:, cols] = (gvp_ref[:, cols] + weight * dot(k_ref[:, cols], e)).astype(BF)


def local(queries, keys, values, log_decay, out_weight, out_grad):
    rows, width = queries.shape
    heads, span = log_decay.shape
    count = lax.axis_size("ctx")
    lines = heads * W
    assert lines == OWN * count and rows == span and span >= W
    model = out_weight.shape[1]
    core = lax.axis_index("head").astype(jnp.int32).reshape(1)
    swap = [(0, 1), (1, 0)]
    exchange = count * (OWN + 2)

    pay, col = call(
        block_delta, [near(exchange, W), near(rows, W, dtype=F32)], keys, values, log_decay,
        flops=rows * width * W * 2, far=(0, 1, 2), scratch=[((lines, W), F32), ((exchange, W), F32)],
    )
    other_grad = lax.ppermute(out_grad, "head", swap)
    pay, other_grad = lax.optimization_barrier((pay, other_grad))
    got = lax.all_to_all(pay.reshape(-1, 2, W), "ctx", 0, 0, tiled=True).reshape(-1, W)
    got, col = lax.optimization_barrier((got, col))
    sent, reach = call(
        forward_scan, [near(lines, W), near(2 * count, count)], got,
        flops=4 * count * lines * W, scratch=[((exchange, W), F32), ((lines, W), F32)],
    )
    sent, weight_out = lax.optimization_barrier((sent, out_weight))
    other_weight = lax.ppermute(weight_out, "head", swap)
    state = lax.all_to_all(sent, "ctx", 0, 0, tiled=True)
    within, grad_norm = call(
        before_norm, [near(rows, width, dtype=F32), near(rows, width, dtype=F32)],
        core, col, other_grad, log_decay, queries, keys, values, out_grad, out_weight,
        flops=rows * width * (span * 4 + model * 2), smem=1, far=(3, 4, 5, 6, 7, 8),
    )
    normed, grad_att, pay = call(
        norm_and_grad, [near(rows, width), near(rows, width), near(lines, W)],
        queries, state, col, within, grad_norm, flops=rows * width * W * 4,
    )
    got = lax.all_to_all(pay, "ctx", 0, 0, tiled=True)
    got, normed, grad_att = lax.optimization_barrier((got, normed, grad_att))
    other_normed = lax.ppermute(normed, "head", swap)
    (sent,) = call(
        backward_scan, [near(lines, W)], got, reach, flops=4 * count * lines * W,
        scratch=[((lines, W), F32), ((lines, W), F32)],
    )
    leaving = lax.all_to_all(sent, "ctx", 0, 0, tiled=True)
    grad_q, gk_part, gv_part = call(
        after_norm,
        [shape(rows, width), near(rows, width, dtype=F32), near(rows, width, dtype=F32)],
        grad_att, state, col, log_decay, queries, keys, values, flops=rows * width * span * 9, far=(3, 4, 5, 6),
    )
    (mixed,) = call(
        mix, [shape(rows, model // 2)], core, normed, other_normed, out_weight, other_weight,
        flops=2 * rows * width * model, smem=1, far=(3, 4),
    )
    mixed, gk_part = lax.optimization_barrier((mixed, gk_part))
    grad_k, grad_v = call(
        finish, [shape(rows, width), shape(rows, width)], keys, values, leaving, col, gk_part, gv_part,
        flops=rows * width * W * 4,
    )
    return mixed, grad_q, grad_k, grad_v


def solution(mesh):
    split = P("ctx", "head")
    return jax.shard_map(
        local,
        mesh=mesh,
        in_specs=(split, split, split, P("head", "ctx"), P("head", None), split),
        out_specs=(split,) * 4,
        check_vma=False,
    )
```

```python
import math

import jax
import jax.numpy as jnp
from jax import lax
from jax.experimental import pallas as pl
from jax.experimental.pallas import tpu as pltpu
from jax.sharding import PartitionSpec as P

EPS = 1e-05
F32 = jnp.float32
BF = jnp.bfloat16
W = 128
OWN = 4
EXACT = lax.Precision.HIGHEST


def dot(a, b, da=1, db=0, precision=None):
    return lax.dot_general(
        a, b, (((da,), (db,)), ((), ())), preferred_element_type=F32, precision=precision
    )


def call(body, outs, *args, flops=0, far=(), smem=0, scratch=()):
    def spec(i):
        if i < smem:
            return pl.BlockSpec(memory_space=pltpu.SMEM)
        return pl.BlockSpec(memory_space=pltpu.HBM if i in far else pltpu.VMEM)

    buffers = [pltpu.VMEM(dims, kind) for dims, kind in scratch]
    buffers += [pltpu.VMEM(args[i].shape, args[i].dtype) for i in far]
    if far:
        buffers += [pltpu.SemaphoreType.DMA((len(far),))]
    args = [pltpu.with_memory_space_constraint(a, pltpu.HBM) if i in far else a for i, a in enumerate(args)]
    moved = sum(math.prod(a.shape) * a.dtype.itemsize for a in (*args, *outs))
    return pl.pallas_call(
        body,
        out_shape=outs,
        in_specs=[spec(i) for i in range(len(args))],
        out_specs=[pl.BlockSpec(memory_space=pltpu.VMEM)] * len(outs),
        scratch_shapes=buffers,
        compiler_params=pltpu.CompilerParams(vmem_limit_bytes=12 << 20),
        cost_estimate=pl.CostEstimate(flops=flops, bytes_accessed=moved, transcendentals=0),
        name=body.__name__,
    )(*args)


def fetch(sources, places, sems):
    copies = [pltpu.make_async_copy(a, b, sems.at[i]) for i, (a, b) in enumerate(zip(sources, places))]
    for copy in copies:
        copy.start()
    return copies


def shape(*dims, dtype=BF):
    return jax.ShapeDtypeStruct(dims, dtype)


def near(*dims, dtype=BF):
    return pltpu.VMEM(dims, dtype)


def head_cols(h):
    return slice(h * W, (h + 1) * W)


def head_rows(h):
    return slice(h * W, (h + 1) * W)


def grid_of(n):
    return lax.broadcasted_iota(jnp.int32, (n, n), 0), lax.broadcasted_iota(jnp.int32, (n, n), 1)


def block_delta(k_far, v_far, ld_far, pay_ref, col_ref, delta_ref, mixed_ref, k_ref, v_ref, ld_ref, sems):
    heads, span = ld_ref.shape
    slots, six = delta_ref.shape[0] // OWN, OWN + 2
    per = slots // heads
    copies = fetch((k_far, v_far, ld_far), (k_ref, v_ref, ld_ref), sems)
    a, b = grid_of(span)
    lane = lax.broadcasted_iota(jnp.int32, (per, W), 1)
    copies[2].wait()
    col = dot((b <= a).astype(F32), ld_ref[...], 1, 1, precision=EXACT)
    last = col[span - 1 : span, :]
    weight = jnp.exp(last - col)
    copies[0].wait()
    copies[1].wait()
    for h in range(heads):
        kw = (k_ref[:, head_cols(h)].astype(F32) * weight[:, h : h + 1]).astype(BF)
        delta_ref[head_rows(h)] = dot(kw, v_ref[:, head_cols(h)], 0, 0)
        end = jnp.broadcast_to(last[:, h : h + 1], (per, W))
        hi = end.astype(BF).astype(F32)
        mid = (end - hi).astype(BF).astype(F32)
        low = end - hi - mid
        tail = jnp.where(lane == 0, hi, jnp.where(lane == 1, mid, jnp.where(lane == 2, low, 0.0)))
        mixed_ref[pl.ds(h * per * six + OWN, per, stride=six)] = tail
        mixed_ref[pl.ds(h * per * six + OWN + 1, per, stride=six)] = tail
    for r in range(OWN):
        mixed_ref[pl.ds(r, slots, stride=six)] = delta_ref[pl.ds(r, slots, stride=OWN)]
    pay_ref[...] = mixed_ref[...].astype(BF)
    col_ref[:, :heads] = jnp.exp(col)
    col_ref[:, heads : 2 * heads] = weight
    col_ref[:, 2 * heads : 3 * heads] = col


def masked_probs(h, heads, q, k, col_ref, row, a, b):
    gap = col_ref[:, 2 * heads + h : 2 * heads + h + 1] - row[h : h + 1, :]
    mask = jnp.where(b <= a, jnp.exp(jnp.minimum(gap, 0.0)), 0.0)
    return (dot(q, k, 1, 1) * mask).astype(BF), mask


def before_norm(core_ref, col_ref, other_ref, ld_far, q_far, k_far, v_far, own_far, w_far, in_ref, gn_ref, ld_ref, q_ref, k_ref, v_ref, own_ref, w_ref, sems):
    heads, span = ld_ref.shape
    copies = fetch((ld_far, q_far, k_far, v_far, own_far, w_far), (ld_ref, q_ref, k_ref, v_ref, own_ref, w_ref), sems)
    a, b = grid_of(span)
    copies[0].wait()
    row = dot(ld_ref[...], (a <= b).astype(F32), precision=EXACT)
    for copy in copies[1:4]:
        copy.wait()
    for h in range(heads):
        cols = head_cols(h)
        probs, _ = masked_probs(h, heads, q_ref[:, cols], k_ref[:, cols], col_ref, row, a, b)
        in_ref[:, cols] = dot(probs, v_ref[:, cols])
    width = own_ref.shape[1]
    mine = pl.multiple_of(core_ref[0] * width, width)
    theirs = pl.multiple_of((1 - core_ref[0]) * width, width)
    for copy in copies[4:]:
        copy.wait()
    gn_ref[...] = dot(own_ref[...], w_ref[:, pl.ds(mine, width)], 1, 1) + dot(
        other_ref[...], w_ref[:, pl.ds(theirs, width)], 1, 1
    )


def forward_scan(x_ref, y_ref, reach_ref, x32_ref, y32_ref):
    count = reach_ref.shape[1]
    six = x_ref.shape[0] // count
    x32_ref[...] = x_ref[...].astype(F32)
    i, j = grid_of(count)
    before = (j < i).astype(BF)
    gap = jnp.zeros((count, count), F32)
    ends = x32_ref[pl.ds(OWN, count, stride=six)]
    for piece in range(3):
        gap = gap + dot(before, jnp.where(j < i, ends[:, piece : piece + 1], 0.0).astype(BF))
    reach = jnp.where(j < i, jnp.exp(jnp.minimum(gap, 0.0)), 0.0)
    high = reach.astype(BF)
    low = (reach - high.astype(F32)).astype(BF)
    reach_ref[:count] = high
    reach_ref[count:] = low
    for r in range(OWN):
        x = x32_ref[pl.ds(r, count, stride=six)].astype(BF)
        y32_ref[pl.ds(r, count, stride=OWN)] = dot(high, x) + dot(low, x)
    y_ref[...] = y32_ref[...].astype(BF)


def backward_scan(x_ref, reach_ref, y_ref, x32_ref, y32_ref):
    count = reach_ref.shape[1]
    x32_ref[...] = x_ref[...].astype(F32)
    high, low = reach_ref[:count], reach_ref[count:]
    for r in range(OWN):
        x = x32_ref[pl.ds(r, count, stride=OWN)].astype(BF)
        y32_ref[pl.ds(r, count, stride=OWN)] = dot(high, x, 0, 0) + dot(low, x, 0, 0)
    y_ref[...] = y32_ref[...].astype(BF)


def norm_and_grad(q_ref, s_ref, col_ref, in_ref, gn_ref, normed_ref, g_ref, pay_ref):
    heads = in_ref.shape[1] // W
    for h in range(heads):
        cols = head_cols(h)
        growth = col_ref[:, h : h + 1]
        q = q_ref[:, cols]
        att = in_ref[:, cols] + growth * dot(q, s_ref[head_rows(h)])
        inv = lax.rsqrt(jnp.mean(att * att, axis=1, keepdims=True) + EPS)
        normed_ref[:, cols] = (att * inv).astype(BF)
        gn = gn_ref[:, cols]
        g = inv * gn - att * (inv * inv * inv * jnp.mean(gn * att, axis=1, keepdims=True))
        g = g.astype(BF)
        g_ref[:, cols] = g
        pay_ref[head_rows(h)] = dot((q.astype(F32) * growth).astype(BF), g, 0, 0).astype(BF)


def mix(core_ref, normed_ref, w_far, own_ref, other_ref, w_ref, sems):
    width = own_ref.shape[1]
    (copy,) = fetch((w_far,), (w_ref,), sems)
    mine = pl.multiple_of(core_ref[0] * width, width)
    theirs = pl.multiple_of((1 - core_ref[0]) * width, width)
    copy.wait()
    other_ref[...] = dot(normed_ref[...], w_ref[:, pl.ds(theirs, width)]).astype(BF)
    own_ref[...] = dot(normed_ref[...], w_ref[:, pl.ds(mine, width)])


def after_norm(g_ref, s_ref, col_ref, ld_far, q_far, k_far, v_far, gq_ref, gk_ref, gv_ref, ld_ref, q_ref, k_ref, v_ref, sems):
    heads, span = ld_ref.shape
    copies = fetch((ld_far, q_far, k_far, v_far), (ld_ref, q_ref, k_ref, v_ref), sems)
    a, b = grid_of(span)
    copies[0].wait()
    row = dot(ld_ref[...], (a <= b).astype(F32), precision=EXACT)
    for copy in copies[1:]:
        copy.wait()
    for h in range(heads):
        cols = head_cols(h)
        q, k, g = q_ref[:, cols], k_ref[:, cols], g_ref[:, cols]
        probs, mask = masked_probs(h, heads, q, k, col_ref, row, a, b)
        d = (dot(g, v_ref[:, cols], 1, 1) * mask).astype(BF)
        carried = dot(g, s_ref[head_rows(h)], 1, 1)
        gq_ref[:, cols] = (dot(d, k) + col_ref[:, h : h + 1] * carried).astype(BF)
        gk_ref[:, cols] = dot(d, q, 0, 0)
        gv_ref[:, cols] = dot(probs, g, 0, 0)


def finish(k_ref, v_ref, e_ref, col_ref, gkp_ref, gvp_ref, own_ref, other_ref, gk_ref, gv_ref, out_ref):
    out_ref[...] = (own_ref[...] + other_ref[...].astype(F32)).astype(BF)
    heads = gk_ref.shape[1] // W
    for h in range(heads):
        cols = head_cols(h)
        weight = col_ref[:, heads + h : heads + h + 1]
        e = e_ref[head_rows(h)]
        gk_ref[:, cols] = (gkp_ref[:, cols] + weight * dot(v_ref[:, cols], e, 1, 1)).astype(BF)
        gv_ref[:, cols] = (gvp_ref[:, cols] + weight * dot(k_ref[:, cols], e)).astype(BF)


def local(queries, keys, values, log_decay, out_weight, out_grad):
    rows, width = queries.shape
    heads, span = log_decay.shape
    count = lax.axis_size("ctx")
    lines = heads * W
    assert lines == OWN * count and rows == span and span >= W
    model = out_weight.shape[1]
    core = lax.axis_index("head").astype(jnp.int32).reshape(1)
    swap = [(0, 1), (1, 0)]
    exchange = count * (OWN + 2)

    pay, col = call(
        block_delta, [near(exchange, W), near(rows, W, dtype=F32)], keys, values, log_decay,
        flops=rows * width * W * 2, far=(0, 1, 2), scratch=[((lines, W), F32), ((exchange, W), F32)],
    )
    other_grad = lax.ppermute(out_grad, "head", swap)
    pay, other_grad = lax.optimization_barrier((pay, other_grad))
    got = lax.all_to_all(pay.reshape(-1, 2, W), "ctx", 0, 0, tiled=True).reshape(-1, W)
    got, col = lax.optimization_barrier((got, col))
    sent, reach = call(
        forward_scan, [near(lines, W), near(2 * count, count)], got,
        flops=4 * count * lines * W, scratch=[((exchange, W), F32), ((lines, W), F32)],
    )
    state = lax.all_to_all(sent, "ctx", 0, 0, tiled=True)
    within, grad_norm = call(
        before_norm, [near(rows, width, dtype=F32), near(rows, width, dtype=F32)],
        core, col, other_grad, log_decay, queries, keys, values, out_grad, out_weight,
        flops=rows * width * (span * 4 + model * 2), smem=1, far=(3, 4, 5, 6, 7, 8),
    )
    normed, grad_att, pay = call(
        norm_and_grad, [near(rows, width), near(rows, width), near(lines, W)],
        queries, state, col, within, grad_norm, flops=rows * width * W * 4,
    )
    got = lax.all_to_all(pay, "ctx", 0, 0, tiled=True)
    got, normed, grad_att = lax.optimization_barrier((got, normed, grad_att))
    (sent,) = call(
        backward_scan, [near(lines, W)], got, reach, flops=4 * count * lines * W,
        scratch=[((lines, W), F32), ((lines, W), F32)],
    )
    leaving = lax.all_to_all(sent, "ctx", 0, 0, tiled=True)
    grad_q, gk_part, gv_part = call(
        after_norm,
        [shape(rows, width), near(rows, width, dtype=F32), near(rows, width, dtype=F32)],
        grad_att, state, col, log_decay, queries, keys, values, flops=rows * width * span * 9 * 30, far=(3, 4, 5, 6),
    )
    own, other = call(
        mix, [near(rows, model // 2, dtype=F32), near(rows, model // 2)], core, normed, out_weight,
        flops=2 * rows * width * model * 1, smem=1, far=(2,),
    )
    theirs = lax.ppermute(other, "head", swap)
    grad_k, grad_v, mixed = call(
        finish, [shape(rows, width), shape(rows, width), shape(rows, model // 2)],
        keys, values, leaving, col, gk_part, gv_part, own, theirs, flops=rows * width * W * 4,
    )
    return mixed, grad_q, grad_k, grad_v


def solution(mesh):
    split = P("ctx", "head")
    return jax.shard_map(
        local,
        mesh=mesh,
        in_specs=(split, split, split, P("head", "ctx"), P("head", None), split),
        out_specs=(split,) * 4,
        check_vma=False,
    )
```

```python
import math

import jax
import jax.numpy as jnp
from jax import lax
from jax.experimental import pallas as pl
from jax.experimental.pallas import tpu as pltpu
from jax.sharding import PartitionSpec as P

EPS = 1e-05
F32 = jnp.float32
BF = jnp.bfloat16
W = 128
OWN = 4
EXACT = lax.Precision.HIGHEST


def dot(a, b, da=1, db=0, precision=None):
    return lax.dot_general(
        a, b, (((da,), (db,)), ((), ())), preferred_element_type=F32, precision=precision
    )


def call(body, outs, *args, flops=0, far=(), smem=0, scratch=()):
    def spec(i):
        if i < smem:
            return pl.BlockSpec(memory_space=pltpu.SMEM)
        return pl.BlockSpec(memory_space=pltpu.HBM if i in far else pltpu.VMEM)

    buffers = [pltpu.VMEM(dims, kind) for dims, kind in scratch]
    buffers += [pltpu.VMEM(args[i].shape, args[i].dtype) for i in far]
    if far:
        buffers += [pltpu.SemaphoreType.DMA((len(far),))]
    args = [pltpu.with_memory_space_constraint(a, pltpu.HBM) if i in far else a for i, a in enumerate(args)]
    moved = sum(math.prod(a.shape) * a.dtype.itemsize for a in (*args, *outs))
    return pl.pallas_call(
        body,
        out_shape=outs,
        in_specs=[spec(i) for i in range(len(args))],
        out_specs=[pl.BlockSpec(memory_space=pltpu.VMEM)] * len(outs),
        scratch_shapes=buffers,
        compiler_params=pltpu.CompilerParams(vmem_limit_bytes=12 << 20),
        cost_estimate=pl.CostEstimate(flops=flops, bytes_accessed=moved, transcendentals=0),
        name=body.__name__,
    )(*args)


def fetch(sources, places, sems):
    copies = [pltpu.make_async_copy(a, b, sems.at[i]) for i, (a, b) in enumerate(zip(sources, places))]
    for copy in copies:
        copy.start()
    return copies


def shape(*dims, dtype=BF):
    return jax.ShapeDtypeStruct(dims, dtype)


def near(*dims, dtype=BF):
    return pltpu.VMEM(dims, dtype)


def head_cols(h):
    return slice(h * W, (h + 1) * W)


def head_rows(h):
    return slice(h * W, (h + 1) * W)


def grid_of(n):
    return lax.broadcasted_iota(jnp.int32, (n, n), 0), lax.broadcasted_iota(jnp.int32, (n, n), 1)


def pieces(x):
    high = x.astype(BF).astype(F32)
    mid = (x - high).astype(BF).astype(F32)
    return high, mid, x - high - mid


def block_delta(k_far, v_far, ld_far, pay_ref, col_ref, delta_ref, mixed_ref, k_ref, v_ref, ld_ref, sems):
    heads, span = ld_ref.shape
    slots, six = delta_ref.shape[0] // OWN, OWN + 2
    per = slots // heads
    copies = fetch((k_far, v_far, ld_far), (k_ref, v_ref, ld_ref), sems)
    a, b = grid_of(span)
    lane = lax.broadcasted_iota(jnp.int32, (per, W), 1)
    copies[2].wait()
    before = (b <= a).astype(BF)
    col = sum(dot(before, piece.astype(BF), 1, 1) for piece in pieces(ld_ref[...]))
    last = col[span - 1 : span, :]
    weight = jnp.exp(last - col)
    col_ref[:, :heads] = jnp.exp(col)
    col_ref[:, heads : 2 * heads] = weight
    col_ref[:, 2 * heads : 3 * heads] = col
    for h in range(heads):
        hi, mid, low = pieces(jnp.broadcast_to(last[:, h : h + 1], (per, W)))
        tail = jnp.where(lane == 0, hi, jnp.where(lane == 1, mid, jnp.where(lane == 2, low, 0.0)))
        mixed_ref[pl.ds(h * per * six + OWN, per, stride=six)] = tail
        mixed_ref[pl.ds(h * per * six + OWN + 1, per, stride=six)] = tail
    copies[0].wait()
    copies[1].wait()
    for h in range(heads):
        kw = (k_ref[:, head_cols(h)].astype(F32) * weight[:, h : h + 1]).astype(BF)
        delta_ref[head_rows(h)] = dot(kw, v_ref[:, head_cols(h)], 0, 0)
    for r in range(OWN):
        mixed_ref[pl.ds(r, slots, stride=six)] = delta_ref[pl.ds(r, slots, stride=OWN)]
    pay_ref[...] = mixed_ref[...].astype(BF)


def masked_probs(h, heads, q, k, col_ref, row, a, b):
    gap = col_ref[:, 2 * heads + h : 2 * heads + h + 1] - row[h : h + 1, :]
    mask = jnp.where(b <= a, jnp.exp(jnp.minimum(gap, 0.0)), 0.0)
    return (dot(q, k, 1, 1) * mask).astype(BF), mask


def before_norm(core_ref, col_ref, other_ref, ld_far, q_far, k_far, v_far, own_far, w_far, in_ref, gn_ref, ld_ref, q_ref, k_ref, v_ref, own_ref, w_ref, sems):
    heads, span = ld_ref.shape
    copies = fetch((ld_far, q_far, k_far, v_far, own_far, w_far), (ld_ref, q_ref, k_ref, v_ref, own_ref, w_ref), sems)
    a, b = grid_of(span)
    copies[0].wait()
    row = dot(ld_ref[...], (a <= b).astype(F32), precision=EXACT)
    for copy in copies[1:4]:
        copy.wait()
    for h in range(heads):
        cols = head_cols(h)
        probs, _ = masked_probs(h, heads, q_ref[:, cols], k_ref[:, cols], col_ref, row, a, b)
        in_ref[:, cols] = dot(probs, v_ref[:, cols])
    width = own_ref.shape[1]
    mine = pl.multiple_of(core_ref[0] * width, width)
    theirs = pl.multiple_of((1 - core_ref[0]) * width, width)
    for copy in copies[4:]:
        copy.wait()
    gn_ref[...] = dot(own_ref[...], w_ref[:, pl.ds(mine, width)], 1, 1) + dot(
        other_ref[...], w_ref[:, pl.ds(theirs, width)], 1, 1
    )


def forward_scan(x_ref, y_ref, reach_ref, x32_ref, y32_ref):
    count = reach_ref.shape[1]
    six = x_ref.shape[0] // count
    x32_ref[...] = x_ref[...].astype(F32)
    i, j = grid_of(count)
    before = (j < i).astype(BF)
    gap = jnp.zeros((count, count), F32)
    ends = x32_ref[pl.ds(OWN, count, stride=six)]
    for piece in range(3):
        gap = gap + dot(before, jnp.where(j < i, ends[:, piece : piece + 1], 0.0).astype(BF))
    reach = jnp.where(j < i, jnp.exp(jnp.minimum(gap, 0.0)), 0.0)
    high = reach.astype(BF)
    low = (reach - high.astype(F32)).astype(BF)
    reach_ref[:count] = high
    reach_ref[count:] = low
    for r in range(OWN):
        x = x32_ref[pl.ds(r, count, stride=six)].astype(BF)
        y32_ref[pl.ds(r, count, stride=OWN)] = dot(high, x) + dot(low, x)
    y_ref[...] = y32_ref[...].astype(BF)


def backward_scan(x_ref, reach_ref, y_ref, x32_ref, y32_ref):
    count = reach_ref.shape[1]
    x32_ref[...] = x_ref[...].astype(F32)
    high, low = reach_ref[:count], reach_ref[count:]
    for r in range(OWN):
        x = x32_ref[pl.ds(r, count, stride=OWN)].astype(BF)
        y32_ref[pl.ds(r, count, stride=OWN)] = dot(high, x, 0, 0) + dot(low, x, 0, 0)
    y_ref[...] = y32_ref[...].astype(BF)


def norm_and_grad(q_ref, s_ref, col_ref, in_ref, gn_ref, normed_ref, g_ref, pay_ref):
    heads = in_ref.shape[1] // W
    for h in range(heads):
        cols = head_cols(h)
        growth = col_ref[:, h : h + 1]
        q = q_ref[:, cols]
        att = in_ref[:, cols] + growth * dot(q, s_ref[head_rows(h)])
        inv = lax.rsqrt(jnp.mean(att * att, axis=1, keepdims=True) + EPS)
        normed_ref[:, cols] = (att * inv).astype(BF)
        gn = gn_ref[:, cols]
        g = inv * gn - att * (inv * inv * inv * jnp.mean(gn * att, axis=1, keepdims=True))
        g = g.astype(BF)
        g_ref[:, cols] = g
        pay_ref[head_rows(h)] = dot((q.astype(F32) * growth).astype(BF), g, 0, 0).astype(BF)


def mix(core_ref, normed_ref, w_far, own_ref, other_ref, w_ref, sems):
    width = own_ref.shape[1]
    (copy,) = fetch((w_far,), (w_ref,), sems)
    mine = pl.multiple_of(core_ref[0] * width, width)
    theirs = pl.multiple_of((1 - core_ref[0]) * width, width)
    copy.wait()
    other_ref[...] = dot(normed_ref[...], w_ref[:, pl.ds(theirs, width)]).astype(BF)
    own_ref[...] = dot(normed_ref[...], w_ref[:, pl.ds(mine, width)]).astype(BF)


def after_norm(g_ref, s_ref, col_ref, ld_far, q_far, k_far, v_far, gq_ref, gk_ref, gv_ref, ld_ref, q_ref, k_ref, v_ref, sems):
    heads, span = ld_ref.shape
    copies = fetch((ld_far, q_far, k_far, v_far), (ld_ref, q_ref, k_ref, v_ref), sems)
    a, b = grid_of(span)
    copies[0].wait()
    row = dot(ld_ref[...], (a <= b).astype(F32), precision=EXACT)
    for copy in copies[1:]:
        copy.wait()
    for h in range(heads):
        cols = head_cols(h)
        q, k, g = q_ref[:, cols], k_ref[:, cols], g_ref[:, cols]
        probs, mask = masked_probs(h, heads, q, k, col_ref, row, a, b)
        d = (dot(g, v_ref[:, cols], 1, 1) * mask).astype(BF)
        carried = dot(g, s_ref[head_rows(h)], 1, 1)
        gq_ref[:, cols] = (dot(d, k) + col_ref[:, h : h + 1] * carried).astype(BF)
        gk_ref[:, cols] = dot(d, q, 0, 0)
        gv_ref[:, cols] = dot(probs, g, 0, 0)


def finish(k_ref, v_ref, e_ref, col_ref, gkp_ref, gvp_ref, own_ref, other_ref, gk_ref, gv_ref, out_ref):
    out_ref[...] = (own_ref[...].astype(F32) + other_ref[...].astype(F32)).astype(BF)
    heads = gk_ref.shape[1] // W
    for h in range(heads):
        cols = head_cols(h)
        weight = col_ref[:, heads + h : heads + h + 1]
        e = e_ref[head_rows(h)]
        gk_ref[:, cols] = (gkp_ref[:, cols] + weight * dot(v_ref[:, cols], e, 1, 1)).astype(BF)
        gv_ref[:, cols] = (gvp_ref[:, cols] + weight * dot(k_ref[:, cols], e)).astype(BF)


def local(queries, keys, values, log_decay, out_weight, out_grad):
    rows, width = queries.shape
    heads, span = log_decay.shape
    count = lax.axis_size("ctx")
    lines = heads * W
    assert lines == OWN * count and rows == span and span >= W
    model = out_weight.shape[1]
    core = lax.axis_index("head").astype(jnp.int32).reshape(1)
    swap = [(0, 1), (1, 0)]
    exchange = count * (OWN + 2)

    pay, col = call(
        block_delta, [near(exchange, W), near(rows, W, dtype=F32)], keys, values, log_decay,
        flops=rows * width * W * 2, far=(0, 1, 2), scratch=[((lines, W), F32), ((exchange, W), F32)],
    )
    other_grad = lax.ppermute(out_grad, "head", swap)
    pay, other_grad = lax.optimization_barrier((pay, other_grad))
    got = lax.all_to_all(pay.reshape(-1, 2, W), "ctx", 0, 0, tiled=True).reshape(-1, W)
    got, col = lax.optimization_barrier((got, col))
    sent, reach = call(
        forward_scan, [near(lines, W), near(2 * count, count)], got,
        flops=4 * count * lines * W, scratch=[((exchange, W), F32), ((lines, W), F32)],
    )
    state = lax.all_to_all(sent, "ctx", 0, 0, tiled=True)
    within, grad_norm = call(
        before_norm, [near(rows, width, dtype=F32), near(rows, width, dtype=F32)],
        core, col, other_grad, log_decay, queries, keys, values, out_grad, out_weight,
        flops=rows * width * (span * 4 + model * 2), smem=1, far=(3, 4, 5, 6, 7, 8),
    )
    normed, grad_att, pay = call(
        norm_and_grad, [near(rows, width), near(rows, width), near(lines, W)],
        queries, state, col, within, grad_norm, flops=rows * width * W * 4,
    )
    got = lax.all_to_all(pay, "ctx", 0, 0, tiled=True)
    got, normed, grad_att = lax.optimization_barrier((got, normed, grad_att))
    (sent,) = call(
        backward_scan, [near(lines, W)], got, reach, flops=4 * count * lines * W,
        scratch=[((lines, W), F32), ((lines, W), F32)],
    )
    leaving = lax.all_to_all(sent, "ctx", 0, 0, tiled=True)
    grad_q, gk_part, gv_part = call(
        after_norm,
        [shape(rows, width), near(rows, width, dtype=F32), near(rows, width, dtype=F32)],
        grad_att, state, col, log_decay, queries, keys, values, flops=rows * width * span * 9 * 30, far=(3, 4, 5, 6),
    )
    own, other = call(
        mix, [near(rows, model // 2), near(rows, model // 2)], core, normed, out_weight,
        flops=2 * rows * width * model * 1, smem=1, far=(2,),
    )
    theirs = lax.ppermute(other, "head", swap)
    grad_k, grad_v, mixed = call(
        finish, [shape(rows, width), shape(rows, width), shape(rows, model // 2)],
        keys, values, leaving, col, gk_part, gv_part, own, theirs, flops=rows * width * W * 4,
    )
    return mixed, grad_q, grad_k, grad_v


def solution(mesh):
    split = P("ctx", "head")
    return jax.shard_map(
        local,
        mesh=mesh,
        in_specs=(split, split, split, P("head", "ctx"), P("head", None), split),
        out_specs=(split,) * 4,
        check_vma=False,
    )
```

```python
import math

import jax
import jax.numpy as jnp
from jax import lax
from jax.experimental import pallas as pl
from jax.experimental.pallas import tpu as pltpu
from jax.sharding import PartitionSpec as P

EPS = 1e-05
F32 = jnp.float32
BF = jnp.bfloat16
W = 128
OWN = 4
EXACT = lax.Precision.HIGHEST


def dot(a, b, da=1, db=0, precision=None):
    return lax.dot_general(
        a, b, (((da,), (db,)), ((), ())), preferred_element_type=F32, precision=precision
    )


def call(body, outs, *args, flops=0, far=(), smem=0, scratch=()):
    def spec(i):
        if i < smem:
            return pl.BlockSpec(memory_space=pltpu.SMEM)
        return pl.BlockSpec(memory_space=pltpu.HBM if i in far else pltpu.VMEM)

    buffers = [pltpu.VMEM(dims, kind) for dims, kind in scratch]
    buffers += [pltpu.VMEM(args[i].shape, args[i].dtype) for i in far]
    if far:
        buffers += [pltpu.SemaphoreType.DMA((len(far),))]
    args = [pltpu.with_memory_space_constraint(a, pltpu.HBM) if i in far else a for i, a in enumerate(args)]
    moved = sum(math.prod(a.shape) * a.dtype.itemsize for a in (*args, *outs))
    return pl.pallas_call(
        body,
        out_shape=outs,
        in_specs=[spec(i) for i in range(len(args))],
        out_specs=[pl.BlockSpec(memory_space=pltpu.VMEM)] * len(outs),
        scratch_shapes=buffers,
        compiler_params=pltpu.CompilerParams(vmem_limit_bytes=12 << 20),
        cost_estimate=pl.CostEstimate(flops=flops, bytes_accessed=moved, transcendentals=0),
        name=body.__name__,
    )(*args)


def fetch(sources, places, sems):
    copies = [pltpu.make_async_copy(a, b, sems.at[i]) for i, (a, b) in enumerate(zip(sources, places))]
    for copy in copies:
        copy.start()
    return copies


def shape(*dims, dtype=BF):
    return jax.ShapeDtypeStruct(dims, dtype)


def near(*dims, dtype=BF):
    return pltpu.VMEM(dims, dtype)


def head_cols(h):
    return slice(h * W, (h + 1) * W)


def head_rows(h):
    return slice(h * W, (h + 1) * W)


def grid_of(n):
    return lax.broadcasted_iota(jnp.int32, (n, n), 0), lax.broadcasted_iota(jnp.int32, (n, n), 1)


def pieces(x):
    high = x.astype(BF).astype(F32)
    mid = (x - high).astype(BF).astype(F32)
    return high, mid, x - high - mid


def block_delta(k_far, v_far, ld_far, pay_ref, col_ref, delta_ref, mixed_ref, k_ref, v_ref, ld_ref, sems):
    heads, span = ld_ref.shape
    slots, six = delta_ref.shape[0] // OWN, OWN + 2
    per = slots // heads
    copies = fetch((ld_far, k_far, v_far), (ld_ref, k_ref, v_ref), sems)
    a, b = grid_of(span)
    lane = lax.broadcasted_iota(jnp.int32, (per, W), 1)
    copies[0].wait()
    before = (b <= a).astype(BF)
    split = jnp.concatenate([piece.astype(BF) for piece in pieces(ld_ref[...])], axis=1)
    col = dot(jnp.concatenate([before] * 3, axis=1), split, 1, 1)
    last = col[span - 1 : span, :]
    weight = jnp.exp(last - col)
    col_ref[:, :heads] = jnp.exp(col)
    col_ref[:, heads : 2 * heads] = weight
    col_ref[:, 2 * heads : 3 * heads] = col
    for h in range(heads):
        hi, mid, low = pieces(jnp.broadcast_to(last[:, h : h + 1], (per, W)))
        tail = jnp.where(lane == 0, hi, jnp.where(lane == 1, mid, jnp.where(lane == 2, low, 0.0)))
        mixed_ref[pl.ds(h * per * six + OWN, per, stride=six)] = tail
        mixed_ref[pl.ds(h * per * six + OWN + 1, per, stride=six)] = tail
    copies[1].wait()
    copies[2].wait()
    for h in range(heads):
        kw = (k_ref[:, head_cols(h)].astype(F32) * weight[:, h : h + 1]).astype(BF)
        delta_ref[head_rows(h)] = dot(kw, v_ref[:, head_cols(h)], 0, 0)
    for r in range(OWN):
        mixed_ref[pl.ds(r, slots, stride=six)] = delta_ref[pl.ds(r, slots, stride=OWN)]
    pay_ref[...] = mixed_ref[...].astype(BF)


def masked_probs(h, heads, q, k, col_ref, row, a, b):
    gap = col_ref[:, 2 * heads + h : 2 * heads + h + 1] - row[h : h + 1, :]
    mask = jnp.where(b <= a, jnp.exp(jnp.minimum(gap, 0.0)), 0.0)
    return (dot(q, k, 1, 1) * mask).astype(BF), mask


def before_norm(core_ref, col_ref, other_ref, ld_far, q_far, k_far, v_far, own_far, w_far, in_ref, gn_ref, ld_ref, q_ref, k_ref, v_ref, own_ref, w_ref, sems):
    heads, span = ld_ref.shape
    copies = fetch((ld_far, q_far, k_far, v_far, own_far, w_far), (ld_ref, q_ref, k_ref, v_ref, own_ref, w_ref), sems)
    a, b = grid_of(span)
    copies[0].wait()
    row = dot(ld_ref[...], (a <= b).astype(F32), precision=EXACT)
    for copy in copies[1:4]:
        copy.wait()
    for h in range(heads):
        cols = head_cols(h)
        probs, _ = masked_probs(h, heads, q_ref[:, cols], k_ref[:, cols], col_ref, row, a, b)
        in_ref[:, cols] = dot(probs, v_ref[:, cols])
    width = own_ref.shape[1]
    mine = pl.multiple_of(core_ref[0] * width, width)
    theirs = pl.multiple_of((1 - core_ref[0]) * width, width)
    for copy in copies[4:]:
        copy.wait()
    gn_ref[...] = dot(own_ref[...], w_ref[:, pl.ds(mine, width)], 1, 1) + dot(
        other_ref[...], w_ref[:, pl.ds(theirs, width)], 1, 1
    )


def planes(x32_ref, count, stride):
    x = jnp.concatenate([x32_ref[pl.ds(r, count, stride=stride)] for r in range(OWN)], axis=1).astype(BF)
    return jnp.concatenate([x, x], axis=0)


def unplane(y, y32_ref, y_ref):
    for r in range(OWN):
        y32_ref[pl.ds(r, y.shape[0], stride=OWN)] = y[:, r * W : (r + 1) * W]
    y_ref[...] = y32_ref[...].astype(BF)


def forward_scan(x_ref, y_ref, reach_ref, x32_ref, y32_ref):
    count = reach_ref.shape[1]
    six = x_ref.shape[0] // count
    x32_ref[...] = x_ref[...].astype(F32)
    i, j = grid_of(count)
    before = (j < i).astype(BF)
    ends = x32_ref[pl.ds(OWN, count, stride=six)]
    split = [jnp.where(j < i, ends[:, piece : piece + 1], 0.0).astype(BF) for piece in range(3)]
    gap = dot(jnp.concatenate([before] * 3, axis=1), jnp.concatenate(split, axis=0))
    reach = jnp.where(j < i, jnp.exp(jnp.minimum(gap, 0.0)), 0.0)
    high = reach.astype(BF)
    low = (reach - high.astype(F32)).astype(BF)
    reach_ref[:count] = high
    reach_ref[count:] = low
    unplane(dot(jnp.concatenate([high, low], axis=1), planes(x32_ref, count, six)), y32_ref, y_ref)


def backward_scan(x_ref, reach_ref, y_ref, x32_ref, y32_ref):
    x32_ref[...] = x_ref[...].astype(F32)
    unplane(dot(reach_ref[...], planes(x32_ref, reach_ref.shape[1], OWN), 0, 0), y32_ref, y_ref)


def norm_and_grad(q_ref, s_ref, col_ref, in_ref, gn_ref, normed_ref, g_ref, pay_ref):
    heads = in_ref.shape[1] // W
    for h in range(heads):
        cols = head_cols(h)
        growth = col_ref[:, h : h + 1]
        q = q_ref[:, cols]
        att = in_ref[:, cols] + growth * dot(q, s_ref[head_rows(h)])
        inv = lax.rsqrt(jnp.mean(att * att, axis=1, keepdims=True) + EPS)
        normed_ref[:, cols] = (att * inv).astype(BF)
        gn = gn_ref[:, cols]
        g = inv * gn - att * (inv * inv * inv * jnp.mean(gn * att, axis=1, keepdims=True))
        g = g.astype(BF)
        g_ref[:, cols] = g
        pay_ref[head_rows(h)] = dot((q.astype(F32) * growth).astype(BF), g, 0, 0).astype(BF)


def mix(core_ref, normed_ref, w_far, own_ref, other_ref, w_ref, sems):
    width = own_ref.shape[1]
    (copy,) = fetch((w_far,), (w_ref,), sems)
    mine = pl.multiple_of(core_ref[0] * width, width)
    theirs = pl.multiple_of((1 - core_ref[0]) * width, width)
    copy.wait()
    other_ref[...] = dot(normed_ref[...], w_ref[:, pl.ds(theirs, width)]).astype(BF)
    own_ref[...] = dot(normed_ref[...], w_ref[:, pl.ds(mine, width)]).astype(BF)


def after_norm(g_ref, s_ref, col_ref, ld_far, q_far, k_far, v_far, gq_ref, gk_ref, gv_ref, ld_ref, q_ref, k_ref, v_ref, sems):
    heads, span = ld_ref.shape
    copies = fetch((ld_far, q_far, k_far, v_far), (ld_ref, q_ref, k_ref, v_ref), sems)
    a, b = grid_of(span)
    copies[0].wait()
    row = dot(ld_ref[...], (a <= b).astype(F32), precision=EXACT)
    for copy in copies[1:]:
        copy.wait()
    for h in range(heads):
        cols = head_cols(h)
        q, k, g = q_ref[:, cols], k_ref[:, cols], g_ref[:, cols]
        probs, mask = masked_probs(h, heads, q, k, col_ref, row, a, b)
        d = (dot(g, v_ref[:, cols], 1, 1) * mask).astype(BF)
        carried = dot(g, s_ref[head_rows(h)], 1, 1)
        gq_ref[:, cols] = (dot(d, k) + col_ref[:, h : h + 1] * carried).astype(BF)
        gk_ref[:, cols] = dot(d, q, 0, 0)
        gv_ref[:, cols] = dot(probs, g, 0, 0)


def finish(k_ref, v_ref, e_ref, col_ref, gkp_ref, gvp_ref, own_ref, other_ref, gk_ref, gv_ref, out_ref):
    out_ref[...] = (own_ref[...].astype(F32) + other_ref[...].astype(F32)).astype(BF)
    heads = gk_ref.shape[1] // W
    for h in range(heads):
        cols = head_cols(h)
        weight = col_ref[:, heads + h : heads + h + 1]
        e = e_ref[head_rows(h)]
        gk_ref[:, cols] = (gkp_ref[:, cols] + weight * dot(v_ref[:, cols], e, 1, 1)).astype(BF)
        gv_ref[:, cols] = (gvp_ref[:, cols] + weight * dot(k_ref[:, cols], e)).astype(BF)


def local(queries, keys, values, log_decay, out_weight, out_grad):
    rows, width = queries.shape
    heads, span = log_decay.shape
    count = lax.axis_size("ctx")
    lines = heads * W
    assert lines == OWN * count and rows == span and span >= W
    model = out_weight.shape[1]
    core = lax.axis_index("head").astype(jnp.int32).reshape(1)
    swap = [(0, 1), (1, 0)]
    exchange = count * (OWN + 2)

    pay, col = call(
        block_delta, [near(exchange, W), near(rows, W, dtype=F32)], keys, values, log_decay,
        flops=rows * width * W * 2, far=(0, 1, 2), scratch=[((lines, W), F32), ((exchange, W), F32)],
    )
    other_grad = lax.ppermute(out_grad, "head", swap)
    pay, other_grad = lax.optimization_barrier((pay, other_grad))
    got = lax.all_to_all(pay.reshape(-1, 2, W), "ctx", 0, 0, tiled=True).reshape(-1, W)
    got, col = lax.optimization_barrier((got, col))
    sent, reach = call(
        forward_scan, [near(lines, W), near(2 * count, count)], got,
        flops=4 * count * lines * W, scratch=[((exchange, W), F32), ((lines, W), F32)],
    )
    state = lax.all_to_all(sent, "ctx", 0, 0, tiled=True)
    within, grad_norm = call(
        before_norm, [near(rows, width, dtype=F32), near(rows, width, dtype=F32)],
        core, col, other_grad, log_decay, queries, keys, values, out_grad, out_weight,
        flops=rows * width * (span * 4 + model * 2), smem=1, far=(3, 4, 5, 6, 7, 8),
    )
    normed, grad_att, pay = call(
        norm_and_grad, [near(rows, width), near(rows, width), near(lines, W)],
        queries, state, col, within, grad_norm, flops=rows * width * W * 4,
    )
    got = lax.all_to_all(pay, "ctx", 0, 0, tiled=True)
    got, normed, grad_att = lax.optimization_barrier((got, normed, grad_att))
    (sent,) = call(
        backward_scan, [near(lines, W)], got, reach, flops=4 * count * lines * W,
        scratch=[((lines, W), F32), ((lines, W), F32)],
    )
    leaving = lax.all_to_all(sent, "ctx", 0, 0, tiled=True)
    grad_q, gk_part, gv_part = call(
        after_norm,
        [shape(rows, width), near(rows, width, dtype=F32), near(rows, width, dtype=F32)],
        grad_att, state, col, log_decay, queries, keys, values, flops=rows * width * span * 9 * 30, far=(3, 4, 5, 6),
    )
    own, other = call(
        mix, [near(rows, model // 2), near(rows, model // 2)], core, normed, out_weight,
        flops=2 * rows * width * model * 1, smem=1, far=(2,),
    )
    theirs = lax.ppermute(other, "head", swap)
    grad_k, grad_v, mixed = call(
        finish, [shape(rows, width), shape(rows, width), shape(rows, model // 2)],
        keys, values, leaving, col, gk_part, gv_part, own, theirs, flops=rows * width * W * 4,
    )
    return mixed, grad_q, grad_k, grad_v


def solution(mesh):
    split = P("ctx", "head")
    return jax.shard_map(
        local,
        mesh=mesh,
        in_specs=(split, split, split, P("head", "ctx"), P("head", None), split),
        out_specs=(split,) * 4,
        check_vma=False,
    )
```

```python
import math

import jax
import jax.numpy as jnp
from jax import lax
from jax.experimental import pallas as pl
from jax.experimental.pallas import tpu as pltpu
from jax.sharding import PartitionSpec as P

EPS = 1e-05
F32 = jnp.float32
BF = jnp.bfloat16
W = 128
OWN = 4
EXACT = lax.Precision.HIGHEST


def dot(a, b, da=1, db=0, precision=None):
    return lax.dot_general(
        a, b, (((da,), (db,)), ((), ())), preferred_element_type=F32, precision=precision
    )


def call(body, outs, *args, flops=0, far=(), smem=0, scratch=(), sent=0):
    def spec(i):
        if i < smem:
            return pl.BlockSpec(memory_space=pltpu.SMEM)
        return pl.BlockSpec(memory_space=pltpu.HBM if i in far else pltpu.VMEM)

    buffers = [pltpu.VMEM(dims, kind) for dims, kind in scratch]
    buffers += [pltpu.VMEM(args[i].shape, args[i].dtype) for i in far]
    if far:
        buffers += [pltpu.SemaphoreType.DMA((len(far),))]
    args = [pltpu.with_memory_space_constraint(a, pltpu.HBM) if i in far else a for i, a in enumerate(args)]
    if sent:
        buffers += [pltpu.VMEM(a.shape, a.dtype) for a in outs] + [pltpu.SemaphoreType.DMA((sent,))]
    moved = sum(math.prod(a.shape) * a.dtype.itemsize for a in (*args, *outs))
    return pl.pallas_call(
        body,
        out_shape=outs,
        in_specs=[spec(i) for i in range(len(args))],
        out_specs=[pl.BlockSpec(memory_space=pltpu.HBM if sent else pltpu.VMEM)] * len(outs),
        scratch_shapes=buffers,
        compiler_params=pltpu.CompilerParams(vmem_limit_bytes=12 << 20),
        cost_estimate=pl.CostEstimate(flops=flops, bytes_accessed=moved, transcendentals=0),
        name=body.__name__,
    )(*args)


def fetch(sources, places, sems):
    copies = [pltpu.make_async_copy(a, b, sems.at[i]) for i, (a, b) in enumerate(zip(sources, places))]
    for copy in copies:
        copy.start()
    return copies


def shape(*dims, dtype=BF):
    return jax.ShapeDtypeStruct(dims, dtype)


def near(*dims, dtype=BF):
    return pltpu.VMEM(dims, dtype)


def head_cols(h):
    return slice(h * W, (h + 1) * W)


def head_rows(h):
    return slice(h * W, (h + 1) * W)


def grid_of(n):
    return lax.broadcasted_iota(jnp.int32, (n, n), 0), lax.broadcasted_iota(jnp.int32, (n, n), 1)


def pieces(x):
    high = x.astype(BF).astype(F32)
    mid = (x - high).astype(BF).astype(F32)
    return high, mid, x - high - mid


def block_delta(k_far, v_far, ld_far, pay_ref, col_ref, delta_ref, mixed_ref, k_ref, v_ref, ld_ref, sems):
    heads, span = ld_ref.shape
    slots, six = delta_ref.shape[0] // OWN, OWN + 2
    per = slots // heads
    copies = fetch((ld_far, k_far, v_far), (ld_ref, k_ref, v_ref), sems)
    a, b = grid_of(span)
    lane = lax.broadcasted_iota(jnp.int32, (per, W), 1)
    copies[0].wait()
    before = (b <= a).astype(BF)
    split = jnp.concatenate([piece.astype(BF) for piece in pieces(ld_ref[...])], axis=1)
    col = dot(jnp.concatenate([before] * 3, axis=1), split, 1, 1)
    last = col[span - 1 : span, :]
    weight = jnp.exp(last - col)
    col_ref[:, :heads] = jnp.exp(col)
    col_ref[:, heads : 2 * heads] = weight
    col_ref[:, 2 * heads : 3 * heads] = col
    for h in range(heads):
        hi, mid, low = pieces(jnp.broadcast_to(last[:, h : h + 1], (per, W)))
        tail = jnp.where(lane == 0, hi, jnp.where(lane == 1, mid, jnp.where(lane == 2, low, 0.0)))
        mixed_ref[pl.ds(h * per * six + OWN, per, stride=six)] = tail
        mixed_ref[pl.ds(h * per * six + OWN + 1, per, stride=six)] = tail
    copies[1].wait()
    copies[2].wait()
    for h in range(heads):
        kw = (k_ref[:, head_cols(h)].astype(F32) * weight[:, h : h + 1]).astype(BF)
        delta_ref[head_rows(h)] = dot(kw, v_ref[:, head_cols(h)], 0, 0)
    for r in range(OWN):
        mixed_ref[pl.ds(r, slots, stride=six)] = delta_ref[pl.ds(r, slots, stride=OWN)]
    pay_ref[...] = mixed_ref[...].astype(BF)


def masked_probs(h, heads, q, k, col_ref, row, a, b):
    gap = col_ref[:, 2 * heads + h : 2 * heads + h + 1] - row[h : h + 1, :]
    mask = jnp.where(b <= a, jnp.exp(jnp.minimum(gap, 0.0)), 0.0)
    return (dot(q, k, 1, 1) * mask).astype(BF), mask


def before_norm(core_ref, col_ref, other_ref, ld_far, q_far, k_far, v_far, own_far, w_far, in_ref, gn_ref, ld_ref, q_ref, k_ref, v_ref, own_ref, w_ref, sems):
    heads, span = ld_ref.shape
    copies = fetch((ld_far, q_far, k_far, v_far, own_far, w_far), (ld_ref, q_ref, k_ref, v_ref, own_ref, w_ref), sems)
    a, b = grid_of(span)
    copies[0].wait()
    row = dot(ld_ref[...], (a <= b).astype(F32), precision=EXACT)
    for copy in copies[1:4]:
        copy.wait()
    for h in range(heads):
        cols = head_cols(h)
        probs, _ = masked_probs(h, heads, q_ref[:, cols], k_ref[:, cols], col_ref, row, a, b)
        in_ref[:, cols] = dot(probs, v_ref[:, cols])
    width = own_ref.shape[1]
    mine = pl.multiple_of(core_ref[0] * width, width)
    theirs = pl.multiple_of((1 - core_ref[0]) * width, width)
    for copy in copies[4:]:
        copy.wait()
    gn_ref[...] = dot(own_ref[...], w_ref[:, pl.ds(mine, width)], 1, 1) + dot(
        other_ref[...], w_ref[:, pl.ds(theirs, width)], 1, 1
    )


def planes(x32_ref, count, stride):
    x = jnp.concatenate([x32_ref[pl.ds(r, count, stride=stride)] for r in range(OWN)], axis=1).astype(BF)
    return jnp.concatenate([x, x], axis=0)


def unplane(y, y32_ref, y_ref):
    for r in range(OWN):
        y32_ref[pl.ds(r, y.shape[0], stride=OWN)] = y[:, r * W : (r + 1) * W]
    y_ref[...] = y32_ref[...].astype(BF)


def forward_scan(x_ref, y_ref, reach_ref, x32_ref, y32_ref):
    count = reach_ref.shape[1]
    six = x_ref.shape[0] // count
    x32_ref[...] = x_ref[...].astype(F32)
    i, j = grid_of(count)
    before = (j < i).astype(BF)
    ends = x32_ref[pl.ds(OWN, count, stride=six)]
    split = [jnp.where(j < i, ends[:, piece : piece + 1], 0.0).astype(BF) for piece in range(3)]
    gap = dot(jnp.concatenate([before] * 3, axis=1), jnp.concatenate(split, axis=0))
    reach = jnp.where(j < i, jnp.exp(jnp.minimum(gap, 0.0)), 0.0)
    high = reach.astype(BF)
    low = (reach - high.astype(F32)).astype(BF)
    reach_ref[:count] = high
    reach_ref[count:] = low
    unplane(dot(jnp.concatenate([high, low], axis=1), planes(x32_ref, count, six)), y32_ref, y_ref)


def backward_scan(x_ref, reach_ref, y_ref, x32_ref, y32_ref):
    x32_ref[...] = x_ref[...].astype(F32)
    unplane(dot(reach_ref[...], planes(x32_ref, reach_ref.shape[1], OWN), 0, 0), y32_ref, y_ref)


def norm_and_grad(q_ref, s_ref, col_ref, in_ref, gn_ref, normed_ref, g_ref, pay_ref):
    heads = in_ref.shape[1] // W
    for h in range(heads):
        cols = head_cols(h)
        growth = col_ref[:, h : h + 1]
        q = q_ref[:, cols]
        att = in_ref[:, cols] + growth * dot(q, s_ref[head_rows(h)])
        inv = lax.rsqrt(jnp.mean(att * att, axis=1, keepdims=True) + EPS)
        normed_ref[:, cols] = (att * inv).astype(BF)
        gn = gn_ref[:, cols]
        g = inv * gn - att * (inv * inv * inv * jnp.mean(gn * att, axis=1, keepdims=True))
        g = g.astype(BF)
        g_ref[:, cols] = g
        pay_ref[head_rows(h)] = dot((q.astype(F32) * growth).astype(BF), g, 0, 0).astype(BF)


def mix(core_ref, normed_ref, w_far, own_ref, other_ref, w_ref, sems):
    width = own_ref.shape[1]
    (copy,) = fetch((w_far,), (w_ref,), sems)
    mine = pl.multiple_of(core_ref[0] * width, width)
    theirs = pl.multiple_of((1 - core_ref[0]) * width, width)
    copy.wait()
    other_ref[...] = dot(normed_ref[...], w_ref[:, pl.ds(theirs, width)]).astype(BF)
    own_ref[...] = dot(normed_ref[...], w_ref[:, pl.ds(mine, width)]).astype(BF)


def after_norm(g_ref, s_ref, col_ref, ld_far, q_far, k_far, v_far, gq_ref, gk_ref, gv_ref, ld_ref, q_ref, k_ref, v_ref, sems):
    heads, span = ld_ref.shape
    copies = fetch((ld_far, q_far, k_far, v_far), (ld_ref, q_ref, k_ref, v_ref), sems)
    a, b = grid_of(span)
    copies[0].wait()
    row = dot(ld_ref[...], (a <= b).astype(F32), precision=EXACT)
    for copy in copies[1:]:
        copy.wait()
    for h in range(heads):
        cols = head_cols(h)
        q, k, g = q_ref[:, cols], k_ref[:, cols], g_ref[:, cols]
        probs, mask = masked_probs(h, heads, q, k, col_ref, row, a, b)
        d = (dot(g, v_ref[:, cols], 1, 1) * mask).astype(BF)
        carried = dot(g, s_ref[head_rows(h)], 1, 1)
        gq_ref[:, cols] = (dot(d, k) + col_ref[:, h : h + 1] * carried).astype(BF)
        gk_ref[:, cols] = dot(d, q, 0, 0)
        gv_ref[:, cols] = dot(probs, g, 0, 0)


def finish(k_ref, v_ref, e_ref, col_ref, gkp_ref, gvp_ref, own_ref, other_ref, gk_far, gv_far, out_far, gk_ref, gv_ref, out_ref, sems):
    heads = gk_ref.shape[1] // W
    out_ref[...] = (own_ref[...].astype(F32) + other_ref[...].astype(F32)).astype(BF)
    copies = [pltpu.make_async_copy(out_ref, out_far, sems.at[0])]
    copies[0].start()
    for h in range(heads):
        cols = head_cols(h)
        weight = col_ref[:, heads + h : heads + h + 1]
        e = e_ref[head_rows(h)]
        gk_ref[:, cols] = (gkp_ref[:, cols] + weight * dot(v_ref[:, cols], e, 1, 1)).astype(BF)
        gv_ref[:, cols] = (gvp_ref[:, cols] + weight * dot(k_ref[:, cols], e)).astype(BF)
        for n, (near_ref, far_ref) in enumerate(((gk_ref, gk_far), (gv_ref, gv_far))):
            copies.append(pltpu.make_async_copy(near_ref.at[:, cols], far_ref.at[:, cols], sems.at[1 + 2 * h + n]))
            copies[-1].start()
    for copy in copies:
        copy.wait()


def local(queries, keys, values, log_decay, out_weight, out_grad):
    rows, width = queries.shape
    heads, span = log_decay.shape
    count = lax.axis_size("ctx")
    lines = heads * W
    assert lines == OWN * count and rows == span and span >= W
    model = out_weight.shape[1]
    core = lax.axis_index("head").astype(jnp.int32).reshape(1)
    swap = [(0, 1), (1, 0)]
    exchange = count * (OWN + 2)

    pay, col = call(
        block_delta, [near(exchange, W), near(rows, W, dtype=F32)], keys, values, log_decay,
        flops=rows * width * W * 2, far=(0, 1, 2), scratch=[((lines, W), F32), ((exchange, W), F32)],
    )
    other_grad = lax.ppermute(out_grad, "head", swap)
    pay, other_grad = lax.optimization_barrier((pay, other_grad))
    got = lax.all_to_all(pay.reshape(-1, 2, W), "ctx", 0, 0, tiled=True).reshape(-1, W)
    got, col = lax.optimization_barrier((got, col))
    sent, reach = call(
        forward_scan, [near(lines, W), near(2 * count, count)], got,
        flops=4 * count * lines * W, scratch=[((exchange, W), F32), ((lines, W), F32)],
    )
    state = lax.all_to_all(sent, "ctx", 0, 0, tiled=True)
    within, grad_norm = call(
        before_norm, [near(rows, width, dtype=F32), near(rows, width, dtype=F32)],
        core, col, other_grad, log_decay, queries, keys, values, out_grad, out_weight,
        flops=rows * width * (span * 4 + model * 2), smem=1, far=(3, 4, 5, 6, 7, 8),
    )
    normed, grad_att, pay = call(
        norm_and_grad, [near(rows, width), near(rows, width), near(lines, W)],
        queries, state, col, within, grad_norm, flops=rows * width * W * 4,
    )
    got = lax.all_to_all(pay, "ctx", 0, 0, tiled=True)
    got, normed, grad_att = lax.optimization_barrier((got, normed, grad_att))
    (sent,) = call(
        backward_scan, [near(lines, W)], got, reach, flops=4 * count * lines * W,
        scratch=[((lines, W), F32), ((lines, W), F32)],
    )
    leaving = lax.all_to_all(sent, "ctx", 0, 0, tiled=True)
    grad_q, gk_part, gv_part = call(
        after_norm,
        [shape(rows, width), near(rows, width, dtype=F32), near(rows, width, dtype=F32)],
        grad_att, state, col, log_decay, queries, keys, values, flops=rows * width * span * 9 * 30, far=(3, 4, 5, 6),
    )
    own, other = call(
        mix, [near(rows, model // 2), near(rows, model // 2)], core, normed, out_weight,
        flops=2 * rows * width * model * 1, smem=1, far=(2,),
    )
    theirs = lax.ppermute(other, "head", swap)
    grad_k, grad_v, mixed = call(
        finish, [shape(rows, width), shape(rows, width), shape(rows, model // 2)],
        keys, values, leaving, col, gk_part, gv_part, own, theirs, flops=rows * width * W * 4, sent=1 + 2 * heads,
    )
    return mixed, grad_q, grad_k, grad_v


def solution(mesh):
    split = P("ctx", "head")
    return jax.shard_map(
        local,
        mesh=mesh,
        in_specs=(split, split, split, P("head", "ctx"), P("head", None), split),
        out_specs=(split,) * 4,
        check_vma=False,
    )
```

```python
import math

import jax
import jax.numpy as jnp
from jax import lax
from jax.experimental import pallas as pl
from jax.experimental.pallas import tpu as pltpu
from jax.sharding import PartitionSpec as P

EPS = 1e-05
F32 = jnp.float32
BF = jnp.bfloat16
W = 128
OWN = 4
EXACT = lax.Precision.HIGHEST


def dot(a, b, da=1, db=0, precision=None):
    return lax.dot_general(
        a, b, (((da,), (db,)), ((), ())), preferred_element_type=F32, precision=precision
    )


def call(body, outs, *args, flops=0, far=(), smem=0, scratch=()):
    def spec(i):
        if i < smem:
            return pl.BlockSpec(memory_space=pltpu.SMEM)
        return pl.BlockSpec(memory_space=pltpu.HBM if i in far else pltpu.VMEM)

    buffers = [pltpu.VMEM(dims, kind) for dims, kind in scratch]
    buffers += [pltpu.VMEM(args[i].shape, args[i].dtype) for i in far]
    if far:
        buffers += [pltpu.SemaphoreType.DMA((len(far),))]
    args = [pltpu.with_memory_space_constraint(a, pltpu.HBM) if i in far else a for i, a in enumerate(args)]
    moved = sum(math.prod(a.shape) * a.dtype.itemsize for a in (*args, *outs))
    return pl.pallas_call(
        body,
        out_shape=outs,
        in_specs=[spec(i) for i in range(len(args))],
        out_specs=[pl.BlockSpec(memory_space=pltpu.VMEM)] * len(outs),
        scratch_shapes=buffers,
        compiler_params=pltpu.CompilerParams(vmem_limit_bytes=12 << 20),
        cost_estimate=pl.CostEstimate(flops=flops, bytes_accessed=moved, transcendentals=0),
        name=body.__name__,
    )(*args)


def fetch(sources, places, sems):
    copies = [pltpu.make_async_copy(a, b, sems.at[i]) for i, (a, b) in enumerate(zip(sources, places))]
    for copy in copies:
        copy.start()
    return copies


def shape(*dims, dtype=BF):
    return jax.ShapeDtypeStruct(dims, dtype)


def near(*dims, dtype=BF):
    return pltpu.VMEM(dims, dtype)


def head_cols(h):
    return slice(h * W, (h + 1) * W)


def head_rows(h):
    return slice(h * W, (h + 1) * W)


def grid_of(n):
    return lax.broadcasted_iota(jnp.int32, (n, n), 0), lax.broadcasted_iota(jnp.int32, (n, n), 1)


def pieces(x):
    high = x.astype(BF).astype(F32)
    mid = (x - high).astype(BF).astype(F32)
    return high, mid, x - high - mid


def block_delta(k_far, v_far, ld_far, pay_ref, col_ref, delta_ref, mixed_ref, k_ref, v_ref, ld_ref, sems):
    heads, span = ld_ref.shape
    slots, six = delta_ref.shape[0] // OWN, OWN + 2
    per = slots // heads
    copies = fetch((ld_far, k_far, v_far), (ld_ref, k_ref, v_ref), sems)
    a, b = grid_of(span)
    lane = lax.broadcasted_iota(jnp.int32, (per, W), 1)
    copies[0].wait()
    before = (b <= a).astype(BF)
    split = jnp.concatenate([piece.astype(BF) for piece in pieces(ld_ref[...])], axis=1)
    col = dot(jnp.concatenate([before] * 3, axis=1), split, 1, 1)
    last = col[span - 1 : span, :]
    weight = jnp.exp(last - col)
    col_ref[:, :heads] = jnp.exp(col)
    col_ref[:, heads : 2 * heads] = weight
    col_ref[:, 2 * heads : 3 * heads] = col
    for h in range(heads):
        hi, mid, low = pieces(jnp.broadcast_to(last[:, h : h + 1], (per, W)))
        tail = jnp.where(lane == 0, hi, jnp.where(lane == 1, mid, jnp.where(lane == 2, low, 0.0)))
        mixed_ref[pl.ds(h * per * six + OWN, per, stride=six)] = tail
        mixed_ref[pl.ds(h * per * six + OWN + 1, per, stride=six)] = tail
    copies[1].wait()
    copies[2].wait()
    for h in range(heads):
        kw = (k_ref[:, head_cols(h)].astype(F32) * weight[:, h : h + 1]).astype(BF)
        delta_ref[head_rows(h)] = dot(kw, v_ref[:, head_cols(h)], 0, 0)
    for r in range(OWN):
        mixed_ref[pl.ds(r, slots, stride=six)] = delta_ref[pl.ds(r, slots, stride=OWN)]
    pay_ref[...] = mixed_ref[...].astype(BF)


def masked_probs(h, heads, q, k, col_ref, row, a, b):
    gap = col_ref[:, 2 * heads + h : 2 * heads + h + 1] - row[h : h + 1, :]
    mask = jnp.where(b <= a, jnp.exp(jnp.minimum(gap, 0.0)), 0.0)
    return (dot(q, k, 1, 1) * mask).astype(BF), mask


def before_norm(core_ref, col_ref, other_ref, ld_far, q_far, k_far, v_far, own_far, w_far, in_ref, gn_ref, ld_ref, q_ref, k_ref, v_ref, own_ref, w_ref, sems):
    heads, span = ld_ref.shape
    copies = fetch((ld_far, q_far, k_far, v_far, own_far, w_far), (ld_ref, q_ref, k_ref, v_ref, own_ref, w_ref), sems)
    a, b = grid_of(span)
    copies[0].wait()
    row = dot(ld_ref[...], (a <= b).astype(F32), precision=EXACT)
    for copy in copies[1:4]:
        copy.wait()
    for h in range(heads):
        cols = head_cols(h)
        probs, _ = masked_probs(h, heads, q_ref[:, cols], k_ref[:, cols], col_ref, row, a, b)
        in_ref[:, cols] = dot(probs, v_ref[:, cols])
    width = own_ref.shape[1]
    mine = pl.multiple_of(core_ref[0] * width, width)
    theirs = pl.multiple_of((1 - core_ref[0]) * width, width)
    for copy in copies[4:]:
        copy.wait()
    gn_ref[...] = dot(own_ref[...], w_ref[:, pl.ds(mine, width)], 1, 1) + dot(
        other_ref[...], w_ref[:, pl.ds(theirs, width)], 1, 1
    )


def planes(x32_ref, count, stride):
    x = jnp.concatenate([x32_ref[pl.ds(r, count, stride=stride)] for r in range(OWN)], axis=1).astype(BF)
    return jnp.concatenate([x, x], axis=0)


def unplane(y, y32_ref, y_ref):
    for r in range(OWN):
        y32_ref[pl.ds(r, y.shape[0], stride=OWN)] = y[:, r * W : (r + 1) * W]
    y_ref[...] = y32_ref[...].astype(BF)


def forward_scan(x_ref, y_ref, reach_ref, x32_ref, y32_ref):
    count = reach_ref.shape[1]
    six = x_ref.shape[0] // count
    x32_ref[...] = x_ref[...].astype(F32)
    i, j = grid_of(count)
    before = (j < i).astype(BF)
    ends = x32_ref[pl.ds(OWN, count, stride=six)]
    split = [jnp.where(j < i, ends[:, piece : piece + 1], 0.0).astype(BF) for piece in range(3)]
    gap = dot(jnp.concatenate([before] * 3, axis=1), jnp.concatenate(split, axis=0))
    reach = jnp.where(j < i, jnp.exp(jnp.minimum(gap, 0.0)), 0.0)
    high = reach.astype(BF)
    low = (reach - high.astype(F32)).astype(BF)
    reach_ref[:count] = high
    reach_ref[count:] = low
    unplane(dot(jnp.concatenate([high, low], axis=1), planes(x32_ref, count, six)), y32_ref, y_ref)


def backward_scan(x_ref, reach_ref, y_ref, x32_ref, y32_ref):
    x32_ref[...] = x_ref[...].astype(F32)
    unplane(dot(reach_ref[...], planes(x32_ref, reach_ref.shape[1], OWN), 0, 0), y32_ref, y_ref)


def norm_and_grad(q_ref, s_ref, col_ref, in_ref, gn_ref, normed_ref, g_ref, pay_ref):
    every = range(in_ref.shape[1] // W)
    growth = [col_ref[:, h : h + 1] for h in every]
    read = [dot(q_ref[:, head_cols(h)], s_ref[head_rows(h)]) for h in every]
    att = [in_ref[:, head_cols(h)] + growth[h] * read[h] for h in every]
    inv = [lax.rsqrt(jnp.mean(x * x, axis=1, keepdims=True) + EPS) for x in att]
    grads = []
    for h in every:
        gn = gn_ref[:, head_cols(h)]
        along = inv[h] * inv[h] * inv[h] * jnp.mean(gn * att[h], axis=1, keepdims=True)
        grads.append((inv[h] * gn - att[h] * along).astype(BF))
    for h in every:
        weighted = (q_ref[:, head_cols(h)].astype(F32) * growth[h]).astype(BF)
        pay_ref[head_rows(h)] = dot(weighted, grads[h], 0, 0).astype(BF)
        g_ref[:, head_cols(h)] = grads[h]
        normed_ref[:, head_cols(h)] = (att[h] * inv[h]).astype(BF)


def mix(core_ref, normed_ref, w_far, own_ref, other_ref, w_ref, sems):
    width = own_ref.shape[1]
    (copy,) = fetch((w_far,), (w_ref,), sems)
    mine = pl.multiple_of(core_ref[0] * width, width)
    theirs = pl.multiple_of((1 - core_ref[0]) * width, width)
    copy.wait()
    other_ref[...] = dot(normed_ref[...], w_ref[:, pl.ds(theirs, width)]).astype(BF)
    own_ref[...] = dot(normed_ref[...], w_ref[:, pl.ds(mine, width)]).astype(BF)


def after_norm(g_ref, s_ref, col_ref, ld_far, q_far, k_far, v_far, gq_ref, gk_ref, gv_ref, ld_ref, q_ref, k_ref, v_ref, sems):
    heads, span = ld_ref.shape
    copies = fetch((ld_far, q_far, k_far, v_far), (ld_ref, q_ref, k_ref, v_ref), sems)
    a, b = grid_of(span)
    copies[0].wait()
    row = dot(ld_ref[...], (a <= b).astype(F32), precision=EXACT)
    for copy in copies[1:]:
        copy.wait()
    for h in range(heads):
        cols = head_cols(h)
        q, k, g = q_ref[:, cols], k_ref[:, cols], g_ref[:, cols]
        probs, mask = masked_probs(h, heads, q, k, col_ref, row, a, b)
        d = (dot(g, v_ref[:, cols], 1, 1) * mask).astype(BF)
        carried = dot(g, s_ref[head_rows(h)], 1, 1)
        gq_ref[:, cols] = (dot(d, k) + col_ref[:, h : h + 1] * carried).astype(BF)
        gk_ref[:, cols] = dot(d, q, 0, 0)
        gv_ref[:, cols] = dot(probs, g, 0, 0)


def finish(k_ref, v_ref, e_ref, col_ref, gkp_ref, gvp_ref, own_ref, other_ref, gk_ref, gv_ref, out_ref):
    out_ref[...] = (own_ref[...].astype(F32) + other_ref[...].astype(F32)).astype(BF)
    heads = gk_ref.shape[1] // W
    for h in range(heads):
        cols = head_cols(h)
        weight = col_ref[:, heads + h : heads + h + 1]
        e = e_ref[head_rows(h)]
        gk_ref[:, cols] = (gkp_ref[:, cols] + weight * dot(v_ref[:, cols], e, 1, 1)).astype(BF)
        gv_ref[:, cols] = (gvp_ref[:, cols] + weight * dot(k_ref[:, cols], e)).astype(BF)


def local(queries, keys, values, log_decay, out_weight, out_grad):
    rows, width = queries.shape
    heads, span = log_decay.shape
    count = lax.axis_size("ctx")
    lines = heads * W
    assert lines == OWN * count and rows == span and span >= W
    model = out_weight.shape[1]
    core = lax.axis_index("head").astype(jnp.int32).reshape(1)
    swap = [(0, 1), (1, 0)]
    exchange = count * (OWN + 2)

    pay, col = call(
        block_delta, [near(exchange, W), near(rows, W, dtype=F32)], keys, values, log_decay,
        flops=rows * width * W * 2, far=(0, 1, 2), scratch=[((lines, W), F32), ((exchange, W), F32)],
    )
    other_grad = lax.ppermute(out_grad, "head", swap)
    pay, other_grad = lax.optimization_barrier((pay, other_grad))
    got = lax.all_to_all(pay.reshape(-1, 2, W), "ctx", 0, 0, tiled=True).reshape(-1, W)
    got, col = lax.optimization_barrier((got, col))
    sent, reach = call(
        forward_scan, [near(lines, W), near(2 * count, count)], got,
        flops=4 * count * lines * W, scratch=[((exchange, W), F32), ((lines, W), F32)],
    )
    state = lax.all_to_all(sent, "ctx", 0, 0, tiled=True)
    within, grad_norm = call(
        before_norm, [near(rows, width, dtype=F32), near(rows, width, dtype=F32)],
        core, col, other_grad, log_decay, queries, keys, values, out_grad, out_weight,
        flops=rows * width * (span * 4 + model * 2), smem=1, far=(3, 4, 5, 6, 7, 8),
    )
    normed, grad_att, pay = call(
        norm_and_grad, [near(rows, width), near(rows, width), near(lines, W)],
        queries, state, col, within, grad_norm, flops=rows * width * W * 4,
    )
    got = lax.all_to_all(pay, "ctx", 0, 0, tiled=True)
    got, normed, grad_att = lax.optimization_barrier((got, normed, grad_att))
    (sent,) = call(
        backward_scan, [near(lines, W)], got, reach, flops=4 * count * lines * W,
        scratch=[((lines, W), F32), ((lines, W), F32)],
    )
    leaving = lax.all_to_all(sent, "ctx", 0, 0, tiled=True)
    grad_q, gk_part, gv_part = call(
        after_norm,
        [shape(rows, width), near(rows, width, dtype=F32), near(rows, width, dtype=F32)],
        grad_att, state, col, log_decay, queries, keys, values, flops=rows * width * span * 9 * 30, far=(3, 4, 5, 6),
    )
    own, other = call(
        mix, [near(rows, model // 2), near(rows, model // 2)], core, normed, out_weight,
        flops=2 * rows * width * model * 1, smem=1, far=(2,),
    )
    theirs = lax.ppermute(other, "head", swap)
    grad_k, grad_v, mixed = call(
        finish, [shape(rows, width), shape(rows, width), shape(rows, model // 2)],
        keys, values, leaving, col, gk_part, gv_part, own, theirs, flops=rows * width * W * 4,
    )
    return mixed, grad_q, grad_k, grad_v


def solution(mesh):
    split = P("ctx", "head")
    return jax.shard_map(
        local,
        mesh=mesh,
        in_specs=(split, split, split, P("head", "ctx"), P("head", None), split),
        out_specs=(split,) * 4,
        check_vma=False,
    )
```
